256 devices in a mesh: lat: 32 (over z, y_hi, core), lon: 8 (over y_lo, x).
Axes of the slice: x: 4, y: 4 (y_hi: 2, y_lo: 2; y = y_hi * 2 + y_lo), z: 8, core: 2. Of those that a mesh axis runs over, the one named last changes fastest.
Arguments:
- state_field: bfloat16 [73, 256, 1024], P(None, 'lat', 'lon'), may hold values from -6 to 6
- support_rows: int32 [128, 5], P('lat'), may hold values from -2 to 2, as said below
- window_bands: int32 [32], replicated, may hold values from 0 to 127, as said below
- conv_weight: bfloat16 [5, 3, 73, 256], replicated, may hold values from -0.1875 to 0.1875
- w_query: bfloat16 [256, 256], replicated
- w_key: bfloat16 [256, 256], replicated
- w_value: bfloat16 [256, 256], replicated, may hold values from -0.375 to 0.375
- w_out: bfloat16 [256, 256], replicated, may hold values from -0.75 to 0.75
Outputs:
- window_out: bfloat16 [32, 512, 256], P('lat', 'lon')
The draws below stay inside these ranges and needn't reach their ends.
Inputs may be any that keep to these rules, and one draw needn't show every extreme that they name: `support_rows`: each row is a permutation of the 5 offsets from -2 to 2. `window_bands`: 32 distinct token bands.
All inputs are finite; a program needn't handle non-finite values.
Results may differ from the reference program's by a relative error of at most 0.019.
Values may be sent and summed in bfloat16 or wider, within the bound.
A program may use at most 64 MiB of HBM per device.

```python
import math
import jax
import jax.numpy as jnp
from jax import lax

C_IN = 73
D = 256
H = 4
KS = 5
NLAT = 128
NLON = 512
QB = 32


def draw_support_rows(key, part):
    branch_keys = jax.random.split(jax.random.fold_in(key, 3), NLAT)

    def one_band(band_key):
        return jax.random.permutation(band_key, KS)
    table = jax.vmap(one_band)(branch_keys)
    return (table - KS // 2).astype(jnp.int32)


def draw_window_bands(key, part):
    inner = jax.random.permutation(jax.random.fold_in(key, 5), NLAT - 2)[:QB - 2] + 1
    chosen = jnp.concatenate([jnp.array([0, NLAT - 1], dtype=jnp.int32), inner.astype(jnp.int32)])
    return jax.random.permutation(jax.random.fold_in(key, 6), chosen).astype(jnp.int32)


def shared_key_matrix(key):
    base = jax.random.normal(jax.random.fold_in(key, 11), (D, D), jnp.float32)
    return jnp.clip(base, -6.0, 6.0) * D ** (-0.5)


def draw_w_key(key, part):
    return shared_key_matrix(key).astype(jnp.bfloat16)


def draw_w_query(key, part):
    base = jax.random.normal(jax.random.fold_in(key, 13), (D, D), jnp.float32)
    drawn = jnp.clip(base, -6.0, 6.0) * (3.0 * D ** (-0.5))
    return drawn.astype(jnp.bfloat16)


def steps_of(own_key, extent, shards, low, high):
    def one(axis_at, parts):
        draws = jax.random.uniform(jax.random.fold_in(jax.random.fold_in(own_key, 6), axis_at), (parts,), jnp.float32, low / len(shards), high / len(shards))
        return jnp.repeat(jnp.exp(draws), extent[axis_at] // parts).reshape((-1,) + (1,) * (len(extent) - axis_at - 1))

    gain = one(*shards[0])
    for cut in shards[1:]:
        gain = gain * one(*cut)
    return gain


def bell_draw(rng, extent, scale, reach, pieces=(), kind=jnp.bfloat16):
    drawn = scale * jax.random.normal(rng, extent, jnp.float32)
    if pieces:
        drawn = drawn * steps_of(rng, extent, pieces, -0.22, 0.18)
    return jnp.clip(drawn, -reach, reach).astype(kind)


def setup_inputs(seed: int = 0) -> dict:
    seeds = jax.random.split(jax.random.key(seed), 9)
    state_field = bell_draw(seeds[0], (C_IN, 2 * NLAT, 2 * NLON), 1.0, 6.0, ((1, 32), (2, 8)))
    support_rows = draw_support_rows(jax.random.fold_in(seeds[8], 71), 0)
    window_bands = draw_window_bands(jax.random.fold_in(seeds[8], 71), 0)
    conv_weight = bell_draw(seeds[3], (KS, 3, C_IN, D), (KS * 3 * C_IN) ** -0.5, 0.1875)
    w_query = draw_w_query(jax.random.fold_in(seeds[8], 71), 0)
    w_key = draw_w_key(jax.random.fold_in(seeds[8], 71), 0)
    w_value = bell_draw(seeds[6], (D, D), D ** -0.5, 0.375)
    w_out = bell_draw(seeds[7], (D, D), (D // 4) ** -0.5, 0.75)
    return {"state_field": state_field, "support_rows": support_rows, "window_bands": window_bands, "conv_weight": conv_weight, "w_query": w_query, "w_key": w_key, "w_value": w_value, "w_out": w_out}


def conv_features(extended, support_rows, conv_weight):
    bands = support_rows.shape[0]
    width = (extended.shape[2] - 1) // 2
    row_index = 2 * jnp.arange(bands, dtype=jnp.int32)[:, None] + support_rows.astype(jnp.int32) + 2
    picked = jnp.take(extended, row_index, axis=1)
    tapped = jnp.stack([picked[..., column_tap:column_tap + 2 * width:2] for column_tap in range(3)], axis=3)
    patches = jnp.transpose(tapped, (1, 4, 2, 3, 0)).reshape(bands * width, -1)
    raw = jnp.dot(patches, conv_weight.reshape(-1, conv_weight.shape[-1]), preferred_element_type=jnp.float32)
    factor = lax.rsqrt(lax.optimization_barrier(jnp.mean(raw * raw, axis=-1, keepdims=True)) + 1e-06)
    return (raw * factor).astype(jnp.bfloat16).reshape(bands, width, -1)

def reference(state_field, support_rows, window_bands, conv_weight, w_query, w_key, w_value, w_out):
    padded = jnp.pad(state_field, ((0, 0), (2, 2), (0, 0)))
    extended = jnp.concatenate([padded[:, :, -1:], padded], axis=2)
    features = conv_features(extended, support_rows, conv_weight)
    flat = features.reshape(-1, D)
    head_size = D // H
    queries = jnp.dot(flat, w_query, preferred_element_type=jnp.float32).astype(jnp.bfloat16).reshape(NLAT, NLON, D)
    keys = jnp.dot(flat, w_key, preferred_element_type=jnp.float32).astype(jnp.bfloat16)
    values = jnp.dot(flat, w_value, preferred_element_type=jnp.float32).astype(jnp.bfloat16)
    keys_wide = keys.astype(jnp.float32).reshape(-1, H, head_size)
    values_wide = values.astype(jnp.float32).reshape(-1, H, head_size)
    window = queries[window_bands.astype(jnp.int32)].reshape(QB * NLON, H, head_size)
    centre = (jnp.arange(NLAT, dtype=jnp.float32) + 0.5) * (math.pi / NLAT) - math.pi / 2
    log_area = jnp.repeat(jnp.log(jnp.cos(centre)), NLON)
    total_rows = QB * NLON
    block_rows = math.gcd(total_rows, 256)
    blocks = window.reshape(total_rows // block_rows, block_rows, H, head_size)
    scale = 1.0 / math.sqrt(head_size)

    def one_block(block_queries):
        scores = jnp.einsum('qhd,khd->qhk', block_queries.astype(jnp.float32), keys_wide) * scale + log_area
        highest = lax.optimization_barrier(jnp.max(scores, axis=-1, keepdims=True))
        weights = jnp.exp(scores - highest)
        totals = lax.optimization_barrier(jnp.sum(weights, axis=-1))
        probs = lax.optimization_barrier(weights.astype(jnp.bfloat16)).astype(jnp.float32)
        mixed = jnp.einsum('qhk,khd->qhd', probs, values_wide)
        return (mixed / totals[..., None]).astype(jnp.bfloat16)
    attended = lax.map(one_block, blocks).reshape(total_rows, D)
    result = jnp.dot(attended, w_out, preferred_element_type=jnp.float32).astype(jnp.bfloat16)
    return result.reshape(QB, NLON, D)
```

```python
import functools
import math

import jax
import jax.numpy as jnp
import numpy as np
from jax import lax
from jax.experimental import pallas as pl
from jax.experimental.pallas import tpu as pltpu
from jax.sharding import PartitionSpec as P

D = 256
H = 4
UP = (4, 3)
DOWN = (3, 4)


def shifted(x, axis, by):
    devices = lax.axis_size(axis)
    return lax.ppermute(x, axis, [(i, (i + by) % devices) for i in range(devices)])


def padded(x, sides, width):
    for axis, dim in sides:
        devices, length = (lax.axis_size(axis), x.shape[dim])
        up = [(i, (i + 1) % devices) for i in range(devices - 1)]
        down = [(j, i) for i, j in up]
        last = lax.slice_in_dim(x, length - width, length, axis=dim)
        leading = lax.slice_in_dim(x, 0, width, axis=dim)
        before = lax.ppermute(last, axis, up)
        after = lax.ppermute(leading, axis, down)
        x = jnp.concatenate([before, x, after], axis=dim)
    return x


def conv_features(extended, support_rows, conv_weight):
    bands = support_rows.shape[0]
    width = (extended.shape[2] - 1) // 2
    row_index = 2 * jnp.arange(bands, dtype=jnp.int32)[:, None] + support_rows + 2
    picked = jnp.take(extended, row_index, axis=1)
    tapped = jnp.stack(
        [picked[..., column_tap : column_tap + 2 * width : 2] for column_tap in range(3)], axis=3
    )
    patches = jnp.transpose(tapped, (1, 4, 2, 3, 0)).reshape(bands * width, -1)
    raw = jnp.dot(
        patches, conv_weight.reshape(-1, conv_weight.shape[-1]), preferred_element_type=jnp.float32
    )
    factor = lax.rsqrt(jnp.mean(raw * raw, axis=-1, keepdims=True) + 1e-06)
    return (raw * factor).astype(jnp.bfloat16)


def remote(src, dst, send, recv, **where):
    return pltpu.make_async_remote_copy(
        src_ref=src, dst_ref=dst, send_sem=send, recv_sem=recv,
        device_id=where, device_id_type=pl.DeviceIdType.MESH)


def greet(peers):
    barrier = pltpu.get_barrier_semaphore()
    for peer in peers:
        pl.semaphore_signal(barrier, inc=1, device_id=peer, device_id_type=pl.DeviceIdType.MESH)
    pl.semaphore_wait(barrier, len(peers))


def gather_kernel(nz, nlon, bands, slot_ref, x_ref, g_ref, q_ref, pick, ysend, yrecv, usend, urecv, dsend, drecv,
                  csend, crecv, qsend, qrecv):
    lat = lax.axis_index("lat")
    lon = lax.axis_index("lon")
    z, yh, c = lat // 4, (lat // 2) % 2, lat % 2

    def at(zz, t, cc):
        side = yh if t == 0 else 1 - yh
        return ((zz + nz) % nz) * 4 + side * 2 + cc

    up, down, across, twin = at(z + 1, 0, c), at(z - 1, 0, c), at(z, 1, c), at(z, 0, 1 - c)
    around = [(lon + k) % nlon for k in range(1, nlon)]
    greet([{"lat": p} for p in (up, down, across, twin)] + [{"lon": p} for p in around])

    waits = []

    def block(index):
        return g_ref.at[pl.ds(index * bands, bands)]

    def source(index, mine):
        return x_ref if mine else block(index)

    def send(index, mine, sends, recvs, to):
        copy = remote(source(index, mine), block(index), sends, recvs, lat=to)
        copy.start()
        waits.append(copy)

    def arrive(index, sends, recvs, peer):
        remote(block(index), block(index), sends, recvs, lat=peer).wait_recv()

    def hop_up(t, s):
        send(at(z - (s - 1), t, c), t == 0 and s == 1, usend.at[t, s - 1], urecv.at[t, s - 1], up)

    def hop_down(t, s):
        send(at(z + (s - 1), t, c), t == 0 and s == 1, dsend.at[t, s - 1], drecv.at[t, s - 1], down)

    twins = []

    def share(dz, t):
        k = len(twins)
        twins.append((dz, t))
        send(at(z + dz, t, c), dz == 0 and t == 0, csend.at[k], crecv.at[k], twin)

    send(lat, True, ysend.at[0], yrecv.at[0], across)
    hop_up(0, 1)
    hop_down(0, 1)
    share(0, 0)
    g_ref[pl.ds(lat * bands, bands)] = x_ref[...]
    arrive(at(z, 1, c), ysend.at[0], yrecv.at[0], across)
    hop_up(1, 1)
    hop_down(1, 1)
    share(0, 1)
    for s in range(1, max(UP + DOWN) + 1):
        for t in range(2):
            if s <= UP[t]:
                arrive(at(z - s, t, c), usend.at[t, s - 1], urecv.at[t, s - 1], down)
                if s < UP[t]:
                    hop_up(t, s + 1)
                share(-s, t)
            if s <= DOWN[t]:
                arrive(at(z + s, t, c), dsend.at[t, s - 1], drecv.at[t, s - 1], up)
                if s < DOWN[t]:
                    hop_down(t, s + 1)
                share(s, t)
    for k, (dz, t) in enumerate(twins):
        arrive(at(z + dz, t, 1 - c), csend.at[k], crecv.at[k], twin)
    chosen = g_ref[slot_ref[lat]]
    pick[...] = chosen
    q_ref[lon] = chosen
    for copy in waits:
        copy.wait_send()
    copies = []
    for k, peer in enumerate(around):
        copy = remote(pick, q_ref.at[lon], qsend.at[k], qrecv.at[k], lon=peer)
        copy.start()
        copies.append(copy)
    for k in range(1, nlon):
        slot = (lon + nlon - k) % nlon
        remote(pick, q_ref.at[slot], qsend.at[k - 1], qrecv.at[k - 1], lon=slot).wait_recv()
    for copy in copies:
        copy.wait_send()


def gather(features, window_bands, bands):
    nlat, nlon = lax.axis_size("lat"), lax.axis_size("lon")
    per = features.shape[1]
    v = pl.BlockSpec(memory_space=pltpu.VMEM)
    dma = pltpu.SemaphoreType.DMA
    nz = nlat // 4
    return pl.pallas_call(
        functools.partial(gather_kernel, nz, nlon, bands),
        out_shape=(
            jax.ShapeDtypeStruct((nlat * bands, per, D), jnp.bfloat16),
            jax.ShapeDtypeStruct((nlon, per, D), jnp.bfloat16),
        ),
        in_specs=[pl.BlockSpec(memory_space=pltpu.SMEM), v],
        out_specs=(v, v),
        scratch_shapes=[
            pltpu.VMEM((per, D), jnp.bfloat16),
            dma((1,)), dma((1,)), dma((2, 4)), dma((2, 4)), dma((2, 4)), dma((2, 4)),
            dma((2 * nz,)), dma((2 * nz,)), dma((nlon - 1,)), dma((nlon - 1,)),
        ],
        compiler_params=pltpu.CompilerParams(collective_id=0, has_side_effects=True, vmem_limit_bytes=24 * 1024 * 1024),
        name="gather_features",
    )(window_bands, features)


def finish_kernel(nlon, o_ref, w_ref, out_ref, held, send, recv):
    lon = lax.axis_index("lon")
    around = [(lon + k) % nlon for k in range(1, nlon)]
    rows = o_ref.shape[0] // nlon
    greet([{"lon": p} for p in around])
    copies = []
    for k, peer in enumerate(around):
        part = o_ref.at[pl.ds(pl.multiple_of(peer * rows, rows), rows), :]
        copy = remote(part, held.at[lon], send.at[k], recv.at[k], lon=peer)
        copy.start()
        copies.append(copy)
    held[lon] = o_ref[pl.ds(pl.multiple_of(lon * rows, rows), rows), :]
    for k in range(1, nlon):
        slot = (lon + nlon - k) % nlon
        remote(held.at[slot], held.at[slot], send.at[k - 1], recv.at[k - 1], lon=slot).wait_recv()
    logs = []
    for i in range(nlon):
        tail = held[i, :, D : D + 128].astype(jnp.float32)
        logs.append([jnp.sum(tail[:, 3 * h : 3 * h + 3], axis=1, keepdims=True) for h in range(H)])
    head = lax.broadcasted_iota(jnp.int32, (rows, D), 1) // (D // H)
    top = [functools.reduce(jnp.maximum, [logs[i][h] for i in range(nlon)]) for h in range(H)]
    share = [[jnp.exp(logs[i][h] - top[h]) for h in range(H)] for i in range(nlon)]
    total = [1.0 / sum(share[i][h] for i in range(nlon)) for h in range(H)]
    mixed = jnp.zeros((rows, D), jnp.float32)
    for i in range(nlon):
        factor = jnp.zeros((rows, D), jnp.float32)
        for h in range(H):
            factor = jnp.where(head == h, share[i][h] * total[h], factor)
        mixed = mixed + factor * held[i, :, 0:D].astype(jnp.float32)
    out_ref[...] = jnp.dot(
        mixed.astype(jnp.bfloat16), w_ref[...], preferred_element_type=jnp.float32
    ).astype(jnp.bfloat16)
    for copy in copies:
        copy.wait_send()


def finish(partial, w_out):
    nlon = lax.axis_size("lon")
    rows = partial.shape[0] // nlon
    v = pl.BlockSpec(memory_space=pltpu.VMEM)
    dma = pltpu.SemaphoreType.DMA
    return pl.pallas_call(
        functools.partial(finish_kernel, nlon),
        out_shape=jax.ShapeDtypeStruct((rows, D), jnp.bfloat16),
        in_specs=[v, v],
        out_specs=v,
        scratch_shapes=[
            pltpu.VMEM((nlon, rows, partial.shape[1]), jnp.bfloat16),
            dma((nlon - 1,)), dma((nlon - 1,)),
        ],
        compiler_params=pltpu.CompilerParams(collective_id=1, has_side_effects=True),
        name="finish",
    )(partial, w_out)


def split3(x):
    a = x.astype(jnp.bfloat16)
    r = x - a.astype(jnp.float32)
    b = r.astype(jnp.bfloat16)
    c = (r - b.astype(jnp.float32)).astype(jnp.bfloat16)
    return a, b, c

def attn_kernel(bk, qc, f_ref, qf_ref, wq_ref, wkv_ref, area_ref, o_ref, ka, va, qa, acc, mx):
    nk = f_ref.shape[0]; nq = qf_ref.shape[0]
    per = nk // area_ref.shape[0]
    rows = 2 * nq
    pb = 512
    def prep(i, c):
        r = pl.ds(pl.multiple_of(i*pb, pb), pb)
        fb = f_ref[r, :]
        kv = jnp.dot(fb, wkv_ref[...], preferred_element_type=jnp.float32).astype(jnp.bfloat16)
        e = area_ref[pl.ds(pl.multiple_of(i*(pb//per), pb//per), pb//per), :]
        e = jnp.broadcast_to(e[:, None, :], (pb//per, per, 128)).reshape(pb, 128).astype(jnp.bfloat16)
        for p in range(2):
            ka[p, r, 0:128] = kv[:, p*128:(p+1)*128]
            ka[p, r, 128:256] = e
            va[p, r, 0:128] = kv[:, 256+p*128:256+(p+1)*128]
            va[p, r, 128:256] = e
        return c
    lax.fori_loop(0, nk//pb, prep, 0)
    q = jnp.dot(qf_ref[...], wq_ref[...], preferred_element_type=jnp.float32).astype(jnp.bfloat16).astype(jnp.float32) * 0.125
    lane = lax.broadcasted_iota(jnp.int32, (nq, 128), 1)
    for p in range(2):
        qp = q[:, p*128:(p+1)*128]
        qa[p, 0:nq, 0:128] = jnp.where(lane < 64, qp, 0.0).astype(jnp.bfloat16)
        qa[p, nq:rows, 0:128] = jnp.where(lane >= 64, qp, 0.0).astype(jnp.bfloat16)
    elane = lax.broadcasted_iota(jnp.int32, (rows, 128), 1)
    ones = jnp.where(elane < 3, 1.0, 0.0)

    def set_shift(p, m):
        a, b, c = split3(m)
        f = lambda t: t.astype(jnp.float32)
        e = ones - jnp.where(elane == 3, f(a), 0.0) - jnp.where(elane == 4, f(b), 0.0) - jnp.where(elane == 5, f(c), 0.0)
        qa[p, :, 128:256] = e.astype(jnp.bfloat16)

    for p in range(2):
        qa[p, :, 128:256] = ones.astype(jnp.bfloat16)
    def scores(p, qr, kr):
        return lax.dot_general(qa[p, qr, :], ka[p, kr, :], (((1,), (1,)), ((), ())), preferred_element_type=jnp.float32)

    sub = pl.ds(nk//2 - 256, 512)
    nqc = rows // qc
    for p in range(2):
        for j in range(rows // 256):
            mx[p, j*256:(j+1)*256, :] = jnp.broadcast_to(jnp.max(scores(p, pl.ds(j*256, 256), sub), axis=1, keepdims=True), (256, 128))
        set_shift(p, mx[p])

    def sweep():
        acc[...] = jnp.zeros_like(acc)
        def body(i, c):
            kr = pl.ds(pl.multiple_of(i*bk, bk), bk)
            for p in range(2):
                for j in range(nqc):
                    qr = pl.ds(j*qc, qc)
                    w = jnp.exp(scores(p, qr, kr)).astype(jnp.bfloat16)
                    acc[p, qr, :] += jnp.dot(w, va[p, kr, :], preferred_element_type=jnp.float32)
            return c
        lax.fori_loop(0, nk//bk, body, 0)
    sweep()
    worst = jnp.maximum(jnp.max(acc[0, :, 131:132]), jnp.max(acc[1, :, 131:132]))

    @pl.when(jnp.logical_not(worst < 1e30))
    def _():
        for p in range(2):
            qa[p, :, 128:256] = ones.astype(jnp.bfloat16)
        mx[...] = jnp.full_like(mx, -jnp.inf)
        def body(i, c):
            kr = pl.ds(pl.multiple_of(i*512, 512), 512)
            p = c
            for p in range(2):
                def qb(j, cc):
                    qr = pl.ds(pl.multiple_of(j*256, 256), 256)
                    s = jnp.max(scores(p, qr, kr), axis=1, keepdims=True)
                    mx[p, qr, :] = jnp.maximum(mx[p, qr, :], s)
                    return cc
                lax.fori_loop(0, rows//256, qb, 0)
            return c
        lax.fori_loop(0, nk//512, body, 0)
        for p in range(2):
            set_shift(p, mx[p])
        sweep()

    tail = jnp.zeros((nq, 128), jnp.float32)
    for p in range(2):
        la = acc[p, 0:nq, 131:132]; lb = acc[p, nq:rows, 131:132]
        o_ref[:, p*128:(p+1)*128] = jnp.where(lane < 64, acc[p, 0:nq, 0:128] / la, acc[p, nq:rows, 0:128] / lb).astype(jnp.bfloat16)
        for s, (l, off) in enumerate(((la, 0), (lb, nq))):
            lse = mx[p, off:off+nq, 0:1] + jnp.log(l)
            pieces = split3(lse)
            h = 2*p + s
            for t in range(3):
                tail = jnp.where(lane == 3*h + t, pieces[t].astype(jnp.float32), tail)
    o_ref[:, 256:384] = tail.astype(jnp.bfloat16)

def area_table(nlat):
    c = (np.arange(nlat, dtype=np.float64) + 0.5) * (math.pi / nlat) - math.pi/2
    a = np.log(np.cos(c)).astype(np.float32)
    t = np.zeros((nlat, 128), np.float32)
    hi = a.astype(jnp.bfloat16).astype(np.float32)
    r = a - hi; mid = r.astype(jnp.bfloat16).astype(np.float32)
    lo = (r-mid).astype(jnp.bfloat16).astype(np.float32)
    t[:,0]=hi; t[:,1]=mid; t[:,2]=lo; t[:,3:6]=1.0
    return t

def attention(f, qf, wq, wk, wv, nlat, bk=2048, qc=256):
    nk, nq = f.shape[0], qf.shape[0]
    wkv = jnp.concatenate([wk, wv], axis=1)
    v = pl.BlockSpec(memory_space=pltpu.VMEM)
    return pl.pallas_call(
        functools.partial(attn_kernel, bk, qc),
        out_shape=jax.ShapeDtypeStruct((nq, 384), jnp.bfloat16),
        in_specs=[v]*5, out_specs=v,
        scratch_shapes=[pltpu.VMEM((2, nk, 256), jnp.bfloat16), pltpu.VMEM((2, nk, 256), jnp.bfloat16),
            pltpu.VMEM((2, 2*nq, 256), jnp.bfloat16), pltpu.VMEM((2, 2*nq, 256), jnp.float32), pltpu.VMEM((2, 2*nq, 128), jnp.float32)],
        compiler_params=pltpu.CompilerParams(vmem_limit_bytes=40*1024*1024),
        name="attend",
    )(f, qf, wq, wkv, jnp.asarray(area_table(nlat)))


def per_device(
    state_field, support_rows, window_bands, conv_weight, w_query, w_key, w_value, w_out
):
    lat_tile = support_rows.shape[0]
    lon_tile = state_field.shape[2] // 2
    band_total = lat_tile * lax.axis_size("lat")
    extended = padded(state_field, (("lat", 1),), 2)
    western = shifted(extended[:, :, -1:], "lon", 1)
    extended = jnp.concatenate([western, extended], axis=2)
    features = conv_features(extended, support_rows, conv_weight)
    everything, chosen = gather(features.reshape(lat_tile, lon_tile, D), window_bands, lat_tile)
    partial = attention(
        everything.reshape(-1, D), chosen.reshape(-1, D), w_query, w_key, w_value, band_total
    )
    return finish(partial, w_out).reshape(1, lon_tile, D)


def solution(mesh):
    return jax.shard_map(
        per_device,
        mesh=mesh,
        in_specs=(P(None, "lat", "lon"), P("lat", None), P(), P(), P(), P(), P(), P()),
        out_specs=P("lat", "lon", None),
        check_vma=False,
    )
```

```python
import functools
import math

import jax
import jax.numpy as jnp
import numpy as np
from jax import lax
from jax.experimental import pallas as pl
from jax.experimental.pallas import tpu as pltpu
from jax.sharding import PartitionSpec as P

D = 256
H = 4
NEAR = 1
PIECES = 2


def remote(src, dst, send, recv, **where):
    return pltpu.make_async_remote_copy(
        src_ref=src, dst_ref=dst, send_sem=send, recv_sem=recv,
        device_id=where, device_id_type=pl.DeviceIdType.MESH)


def greet(peers):
    barrier = pltpu.get_barrier_semaphore()
    for peer in peers:
        pl.semaphore_signal(barrier, inc=1, device_id=peer, device_id_type=pl.DeviceIdType.MESH)
    pl.semaphore_wait(barrier, len(peers))


def ring(nz, near, n, x_ref, g_ref, sems, between):
    ys, yr, us, ur, ds, dr, cs, cr = sems
    bands = x_ref.shape[0]
    w = bands // n
    half = nz // 2
    lat = lax.axis_index("lat")
    z, yh, c = lat // 4, (lat // 2) % 2, lat % 2

    def at(zz, t, cc):
        return ((zz + nz) % nz) * 4 + (yh if t == 0 else 1 - yh) * 2 + cc

    up, down, across, twin = at(z + 1, 0, c), at(z - 1, 0, c), at(z, 1, c), at(z, 0, 1 - c)
    waits, shared, crossing = [], [], {}

    def block(i, p):
        return g_ref.at[pl.ds(i * bands + p * w, w)]

    def send(dz, t, p, sends, recvs, to):
        i = at(z + dz, t, c)
        source = x_ref.at[pl.ds(p * w, w)] if dz == 0 and t == 0 else block(i, p)
        copy = remote(source, block(i, p), sends, recvs, lat=to)
        copy.start()
        waits.append(copy)

    def arrive(dz, t, cc, p, sends, recvs, peer):
        i = at(z + dz, t, cc)
        remote(block(i, p), block(i, p), sends, recvs, lat=peer).wait_recv()

    def limits(t, p):
        return (half, nz - 1 - half) if (t + p) % 2 == 0 else (nz - 1 - half, half)

    def hop(d, p, t, s):
        if s <= limits(t, p)[d]:
            if d == 0:
                send(1 - s, t, p, us.at[p, t, s - 1], ur.at[p, t, s - 1], up)
            else:
                send(s - 1, t, p, ds.at[p, t, s - 1], dr.at[p, t, s - 1], down)

    def landed(d, p, t, s):
        if d == 0:
            arrive(-s, t, c, p, us.at[p, t, s - 1], ur.at[p, t, s - 1], down)
        else:
            arrive(s, t, c, p, ds.at[p, t, s - 1], dr.at[p, t, s - 1], up)
        hop(d, p, t, s + 1)

    def share(dz, t, p):
        k = len(shared)
        shared.append((dz, t, p))
        send(dz, t, p, cs.at[k], cr.at[k], twin)

    def cross(dz, p):
        k = len(crossing)
        crossing[dz, p] = k
        send(dz, 0, p, ys.at[k], yr.at[k], across)

    def over(s):
        for p in range(n):
            for dz in (0,) if s == 0 else (-s, s):
                k = crossing[dz, p]
                arrive(dz, 1, c, p, ys.at[k], yr.at[k], across)
                if dz == -near:
                    hop(0, p, 1, near + 1)
                if dz == near:
                    hop(1, p, 1, near + 1)
                share(dz, 1, p)

    def own(s):
        for p in range(n):
            for d in range(2):
                if s <= limits(0, p)[d]:
                    dz = s if d else -s
                    landed(d, p, 0, s)
                    if s <= near:
                        cross(dz, p)
                    share(dz, 0, p)

    def far(s):
        for p in range(n):
            for d in range(2):
                if s <= limits(1, p)[d]:
                    landed(d, p, 1, s)
                    share(s if d else -s, 1, p)

    for p in range(n):
        cross(0, p)
        hop(0, p, 0, 1)
        hop(1, p, 0, 1)
    for p in range(n):
        share(0, 0, p)
    g_ref[pl.ds(lat * bands, bands)] = x_ref[...]
    between()
    for s in range(half):
        own(s + 1)
        if s <= near:
            over(s)
        else:
            far(s)
    far(half)
    for k, (dz, t, p) in enumerate(shared):
        arrive(dz, t, 1 - c, p, cs.at[k], cr.at[k], twin)
    return waits


def encode_kernel(
    nlat, nlon, slot_ref, rows_ref, xt_ref, conv_ref, wkv_ref, area_ref,
    q_ref, kv_ref, e_ref,
    g_ref, x_ref, ext, taps, pick, hsend, hrecv, ys, yr, us, ur, ds, dr, cs, cr, qsend, qrecv,
):
    lat = lax.axis_index("lat")
    lon = lax.axis_index("lon")
    nz = nlat // 4
    high, cols, channels = xt_ref.shape
    bands, wide = x_ref.shape[0], x_ref.shape[1]
    z, yh, c = lat // 4, (lat // 2) % 2, lat % 2
    north, south = (lat + nlat - 1) % nlat, (lat + 1) % nlat
    west, east = (lon + nlon - 1) % nlon, (lon + 1) % nlon
    around = [(lon + k) % nlon for k in range(1, nlon)]
    column = z * 4 + yh * 2
    greet(
        [{"lat": p} for p in (
            ((z + 1) % nz) * 4 + yh * 2 + c,
            ((z + nz - 1) % nz) * 4 + yh * 2 + c,
            z * 4 + (1 - yh) * 2 + c,
            column + 1 - c,
            north, south,
        )]
        + [{"lon": p} for p in around]
        + [{"lat": a, "lon": b} for a in (north, south) for b in (west, east)]
    )
    strip = 16
    body, edge = pl.ds(0, cols), pl.ds(cols, strip)
    inner = pl.ds(cols - strip, strip)
    first, last = pl.ds(0, 2), pl.ds(high - 2, 2)
    below, above = pl.ds(0, 2), pl.ds(high + 2, 2)
    halo = [
        remote(xt_ref.at[last], ext.at[below, body], hsend.at[0], hrecv.at[0], lat=south),
        remote(xt_ref.at[first], ext.at[above, body], hsend.at[1], hrecv.at[1], lat=north),
        remote(xt_ref.at[:, inner], ext.at[pl.ds(2, high), edge], hsend.at[2], hrecv.at[2], lon=east),
        remote(xt_ref.at[last, inner], ext.at[below, edge], hsend.at[3], hrecv.at[3], lat=south, lon=east),
        remote(xt_ref.at[first, inner], ext.at[above, edge], hsend.at[4], hrecv.at[4], lat=north, lon=east),
    ]
    for copy in halo:
        copy.start()
    ext[2 : high + 2, 0:cols, :] = xt_ref[...]
    at_row = lax.broadcasted_iota(jnp.int32, (3 * wide, cols + strip), 0)
    at_col = lax.broadcasted_iota(jnp.int32, (3 * wide, cols + strip), 1)
    target = 2 * (at_row % wide) + at_row // wide - 1
    target = jnp.where(target < 0, cols + strip - 1, target)
    pickup = jnp.where(at_col == target, 1.0, 0.0).astype(jnp.bfloat16)
    for copy in halo:
        copy.wait_recv()
    keep_low = jnp.where(lat > 0, 1.0, 0.0)
    keep_high = jnp.where(lat < nlat - 1, 1.0, 0.0)
    for r in range(high + 4):
        tap = jnp.dot(pickup, ext[r], preferred_element_type=jnp.float32)
        if r < 2:
            tap = tap * keep_low
        if r >= high + 2:
            tap = tap * keep_high
        taps[r] = tap.astype(jnp.bfloat16)
    raw = jnp.zeros((bands * wide, D), jnp.float32)
    for k in range(rows_ref.shape[1]):
        found = [taps[2 * i + 2 + rows_ref[i, k]] for i in range(bands)]
        for t in range(3):
            part = jnp.concatenate([f[t * wide : (t + 1) * wide] for f in found], axis=0)
            raw = raw + jnp.dot(part, conv_ref[k, t], preferred_element_type=jnp.float32)
    factor = lax.rsqrt(jnp.mean(raw * raw, axis=-1, keepdims=True) + 1e-06)
    x_ref[...] = (raw * factor).astype(jnp.bfloat16).reshape(bands, wide, D)
    for copy in halo:
        copy.wait_send()

    def between():
        e_ref[...] = jnp.broadcast_to(
            area_ref[...][:, None, :], e_ref.shape
        ).astype(jnp.bfloat16)

    waits = ring(nz, NEAR, PIECES, x_ref, g_ref, (ys, yr, us, ur, ds, dr, cs, cr), between)
    chosen = g_ref[slot_ref[lat]]
    pick[...] = chosen
    q_ref[lon] = chosen
    for copy in waits:
        copy.wait_send()
    copies = []
    for k, peer in enumerate(around):
        copy = remote(pick, q_ref.at[lon], qsend.at[k], qrecv.at[k], lon=peer)
        copy.start()
        copies.append(copy)
    group = 8

    def project(i, carry):
        rows = g_ref[pl.ds(i * group, group)].reshape(group * wide, D)
        kv_ref[pl.ds(pl.multiple_of(i * group * wide, group * wide), group * wide), :] = jnp.dot(
            rows, wkv_ref[...], preferred_element_type=jnp.float32
        ).astype(jnp.bfloat16)
        return carry

    lax.fori_loop(0, g_ref.shape[0] // group, project, 0)
    for k in range(1, nlon):
        slot = (lon + nlon - k) % nlon
        remote(pick, q_ref.at[slot], qsend.at[k - 1], qrecv.at[k - 1], lon=slot).wait_recv()
    for copy in copies:
        copy.wait_send()


def encode(window_bands, support_rows, state_field, conv_weight, w_key, w_value):
    nlat, nlon = lax.axis_size("lat"), lax.axis_size("lon")
    bands = support_rows.shape[0]
    channels, high, cols = state_field.shape
    wide = cols // 2
    wkv = jnp.concatenate([w_key, w_value], axis=1)
    v = pl.BlockSpec(memory_space=pltpu.VMEM)
    s = pl.BlockSpec(memory_space=pltpu.SMEM)
    dma = pltpu.SemaphoreType.DMA
    n, nz, total = PIECES, nlat // 4, nlat * bands
    ring_sems = [dma(((2 * NEAR + 1) * n,))] * 2 + [dma((n, 2, nz // 2))] * 4 + [dma((2 * nz * n,))] * 2
    return pl.pallas_call(
        functools.partial(encode_kernel, nlat, nlon),
        out_shape=(
            jax.ShapeDtypeStruct((nlon, wide, D), jnp.bfloat16),
            jax.ShapeDtypeStruct((total * wide, 2 * D), jnp.bfloat16),
            jax.ShapeDtypeStruct((total, wide, 128), jnp.bfloat16),
        ),
        in_specs=[s, s, v, v, v, v],
        out_specs=(v, v, v),
        scratch_shapes=[
            pltpu.VMEM((total, wide, D), jnp.bfloat16),
            pltpu.VMEM((bands, wide, D), jnp.bfloat16),
            pltpu.VMEM((high + 4, cols + 16, channels), jnp.bfloat16),
            pltpu.VMEM((high + 4, 3 * wide, channels), jnp.bfloat16),
            pltpu.VMEM((wide, D), jnp.bfloat16),
            dma((5,)), dma((5,)),
        ] + ring_sems + [dma((nlon - 1,)), dma((nlon - 1,))],
        compiler_params=pltpu.CompilerParams(
            collective_id=0, has_side_effects=True, vmem_limit_bytes=30 * 1024 * 1024
        ),
        name="encode",
    )(
        window_bands, support_rows, jnp.transpose(state_field, (1, 2, 0)), conv_weight, wkv,
        jnp.asarray(area_table(total)),
    )


def finish_kernel(nlon, o_ref, w_ref, out_ref, held, send, recv):
    lon = lax.axis_index("lon")
    around = [(lon + k) % nlon for k in range(1, nlon)]
    rows = o_ref.shape[0] // nlon
    greet([{"lon": p} for p in around])
    copies = []
    for k, peer in enumerate(around):
        part = o_ref.at[pl.ds(pl.multiple_of(peer * rows, rows), rows), :]
        copy = remote(part, held.at[lon], send.at[k], recv.at[k], lon=peer)
        copy.start()
        copies.append(copy)
    held[lon] = o_ref[pl.ds(pl.multiple_of(lon * rows, rows), rows), :]
    for k in range(1, nlon):
        slot = (lon + nlon - k) % nlon
        remote(held.at[slot], held.at[slot], send.at[k - 1], recv.at[k - 1], lon=slot).wait_recv()
    logs = []
    for i in range(nlon):
        tail = held[i, :, D : D + 128].astype(jnp.float32)
        logs.append([jnp.sum(tail[:, 3 * h : 3 * h + 3], axis=1, keepdims=True) for h in range(H)])
    head = lax.broadcasted_iota(jnp.int32, (rows, D), 1) // (D // H)
    top = [functools.reduce(jnp.maximum, [logs[i][h] for i in range(nlon)]) for h in range(H)]
    share = [[jnp.exp(logs[i][h] - top[h]) for h in range(H)] for i in range(nlon)]
    total = [1.0 / sum(share[i][h] for i in range(nlon)) for h in range(H)]
    mixed = jnp.zeros((rows, D), jnp.float32)
    for i in range(nlon):
        factor = jnp.zeros((rows, D), jnp.float32)
        for h in range(H):
            factor = jnp.where(head == h, share[i][h] * total[h], factor)
        mixed = mixed + factor * held[i, :, 0:D].astype(jnp.float32)
    out_ref[...] = jnp.dot(
        mixed.astype(jnp.bfloat16), w_ref[...], preferred_element_type=jnp.float32
    ).astype(jnp.bfloat16)
    for copy in copies:
        copy.wait_send()


def finish(partial, w_out):
    nlon = lax.axis_size("lon")
    rows = partial.shape[0] // nlon
    v = pl.BlockSpec(memory_space=pltpu.VMEM)
    dma = pltpu.SemaphoreType.DMA
    return pl.pallas_call(
        functools.partial(finish_kernel, nlon),
        out_shape=jax.ShapeDtypeStruct((rows, D), jnp.bfloat16),
        in_specs=[v, v],
        out_specs=v,
        scratch_shapes=[
            pltpu.VMEM((nlon, rows, partial.shape[1]), jnp.bfloat16),
            dma((nlon - 1,)), dma((nlon - 1,)),
        ],
        compiler_params=pltpu.CompilerParams(collective_id=1, has_side_effects=True),
        name="finish",
    )(partial, w_out)


def split3(x):
    a = x.astype(jnp.bfloat16)
    r = x - a.astype(jnp.float32)
    b = r.astype(jnp.bfloat16)
    c = (r - b.astype(jnp.float32)).astype(jnp.bfloat16)
    return a, b, c

def attn_kernel(bk, qc, kv_ref, e_ref, qf_ref, wq_ref, o_ref, qa, acc, mx):
    nk = kv_ref.shape[0]
    nq = qf_ref.shape[0]
    rows = 2 * nq
    q = jnp.dot(qf_ref[...], wq_ref[...], preferred_element_type=jnp.float32).astype(jnp.bfloat16).astype(jnp.float32) * 0.125
    lane = lax.broadcasted_iota(jnp.int32, (nq, 128), 1)
    for p in range(2):
        qp = q[:, p*128:(p+1)*128]
        qa[p, 0:nq, 0:128] = jnp.where(lane < 64, qp, 0.0).astype(jnp.bfloat16)
        qa[p, nq:rows, 0:128] = jnp.where(lane >= 64, qp, 0.0).astype(jnp.bfloat16)
    elane = lax.broadcasted_iota(jnp.int32, (rows, 128), 1)
    ones = jnp.where(elane < 3, 1.0, 0.0)

    def set_shift(p, m):
        a, b, c = split3(m)
        f = lambda t: t.astype(jnp.float32)
        e = ones - jnp.where(elane == 3, f(a), 0.0) - jnp.where(elane == 4, f(b), 0.0) - jnp.where(elane == 5, f(c), 0.0)
        qa[p, :, 128:256] = e.astype(jnp.bfloat16)

    for p in range(2):
        qa[p, :, 128:256] = ones.astype(jnp.bfloat16)
    def keyed(p, kr):
        return jnp.concatenate([kv_ref[kr, p * 128 : (p + 1) * 128], e_ref[kr, :]], axis=1)

    def valued(p, kr):
        return jnp.concatenate([kv_ref[kr, D + p * 128 : D + (p + 1) * 128], e_ref[kr, :]], axis=1)

    def scores(p, qr, kr):
        return lax.dot_general(
            qa[p, qr, :], keyed(p, kr), (((1,), (1,)), ((), ())), preferred_element_type=jnp.float32
        )

    sub = pl.ds(nk//2 - 256, 512)
    nqc = rows // qc
    for p in range(2):
        for j in range(rows // 256):
            mx[p, j*256:(j+1)*256, :] = jnp.broadcast_to(jnp.max(scores(p, pl.ds(j*256, 256), sub), axis=1, keepdims=True), (256, 128))
        set_shift(p, mx[p])

    def sweep():
        acc[...] = jnp.zeros_like(acc)
        def body(i, c):
            kr = pl.ds(pl.multiple_of(i*bk, bk), bk)
            for p in range(2):
                for j in range(nqc):
                    qr = pl.ds(j*qc, qc)
                    w = jnp.exp(scores(p, qr, kr)).astype(jnp.bfloat16)
                    acc[p, qr, :] += jnp.dot(w, valued(p, kr), preferred_element_type=jnp.float32)
            return c
        lax.fori_loop(0, nk//bk, body, 0)
    sweep()
    worst = jnp.maximum(jnp.max(acc[0, :, 131:132]), jnp.max(acc[1, :, 131:132]))

    @pl.when(jnp.logical_not(worst < 1e30))
    def _():
        for p in range(2):
            qa[p, :, 128:256] = ones.astype(jnp.bfloat16)
        mx[...] = jnp.full_like(mx, -jnp.inf)
        def body(i, c):
            kr = pl.ds(pl.multiple_of(i*512, 512), 512)
            p = c
            for p in range(2):
                def qb(j, cc):
                    qr = pl.ds(pl.multiple_of(j*256, 256), 256)
                    s = jnp.max(scores(p, qr, kr), axis=1, keepdims=True)
                    mx[p, qr, :] = jnp.maximum(mx[p, qr, :], s)
                    return cc
                lax.fori_loop(0, rows//256, qb, 0)
            return c
        lax.fori_loop(0, nk//512, body, 0)
        for p in range(2):
            set_shift(p, mx[p])
        sweep()

    tail = jnp.zeros((nq, 128), jnp.float32)
    for p in range(2):
        la = acc[p, 0:nq, 131:132]; lb = acc[p, nq:rows, 131:132]
        o_ref[:, p*128:(p+1)*128] = jnp.where(lane < 64, acc[p, 0:nq, 0:128] / la, acc[p, nq:rows, 0:128] / lb).astype(jnp.bfloat16)
        for s, (l, off) in enumerate(((la, 0), (lb, nq))):
            lse = mx[p, off:off+nq, 0:1] + jnp.log(l)
            pieces = split3(lse)
            h = 2*p + s
            for t in range(3):
                tail = jnp.where(lane == 3*h + t, pieces[t].astype(jnp.float32), tail)
    o_ref[:, 256:384] = tail.astype(jnp.bfloat16)

def area_table(nlat):
    c = (np.arange(nlat, dtype=np.float64) + 0.5) * (math.pi / nlat) - math.pi/2
    a = np.log(np.cos(c)).astype(np.float32)
    t = np.zeros((nlat, 128), np.float32)
    hi = a.astype(jnp.bfloat16).astype(np.float32)
    r = a - hi; mid = r.astype(jnp.bfloat16).astype(np.float32)
    lo = (r-mid).astype(jnp.bfloat16).astype(np.float32)
    t[:,0]=hi; t[:,1]=mid; t[:,2]=lo; t[:,3:6]=1.0
    return t

def attention(kv, e, qf, wq, bk=2048, qc=256):
    nq = qf.shape[0]
    v = pl.BlockSpec(memory_space=pltpu.VMEM)
    return pl.pallas_call(
        functools.partial(attn_kernel, bk, qc),
        out_shape=jax.ShapeDtypeStruct((nq, 384), jnp.bfloat16),
        in_specs=[v] * 4,
        out_specs=v,
        scratch_shapes=[
            pltpu.VMEM((2, 2 * nq, D), jnp.bfloat16),
            pltpu.VMEM((2, 2 * nq, D), jnp.float32),
            pltpu.VMEM((2, 2 * nq, 128), jnp.float32),
        ],
        compiler_params=pltpu.CompilerParams(vmem_limit_bytes=30 * 1024 * 1024),
        name="attend",
    )(kv, e, qf, wq)


def per_device(
    state_field, support_rows, window_bands, conv_weight, w_query, w_key, w_value, w_out
):
    lat_tile = support_rows.shape[0]
    lon_tile = state_field.shape[2] // 2
    chosen, kv, e = encode(
        window_bands, support_rows, state_field, conv_weight, w_key, w_value
    )
    partial = attention(kv, e.reshape(kv.shape[0], 128), chosen.reshape(-1, D), w_query)
    return finish(partial, w_out).reshape(1, lon_tile, D)


def solution(mesh):
    return jax.shard_map(
        per_device,
        mesh=mesh,
        in_specs=(P(None, "lat", "lon"), P("lat", None), P(), P(), P(), P(), P(), P()),
        out_specs=P("lat", "lon", None),
        check_vma=False,
    )
```

```python
import functools
import math

import jax
import jax.numpy as jnp
import numpy as np
from jax import lax
from jax.experimental import pallas as pl
from jax.experimental.pallas import tpu as pltpu
from jax.sharding import PartitionSpec as P

D = 256
H = 4
NEAR = 1
PIECES = 2
BLOCK_KEYS = 2048


def remote(src, dst, send, recv, **where):
    return pltpu.make_async_remote_copy(
        src_ref=src, dst_ref=dst, send_sem=send, recv_sem=recv,
        device_id=where, device_id_type=pl.DeviceIdType.MESH)


def greet(peers):
    barrier = pltpu.get_barrier_semaphore()
    for peer in peers:
        pl.semaphore_signal(barrier, inc=1, device_id=peer, device_id_type=pl.DeviceIdType.MESH)
    pl.semaphore_wait(barrier, len(peers))


def ring(nz, near, n, x_ref, g_ref, sems, between):
    ys, yr, us, ur, ds, dr, cs, cr = sems
    bands = x_ref.shape[0]
    w = bands // n
    half = nz // 2
    lat = lax.axis_index("lat")
    z, yh, c = lat // 4, (lat // 2) % 2, lat % 2

    def at(zz, t, cc):
        return ((zz + nz) % nz) * 4 + (yh if t == 0 else 1 - yh) * 2 + cc

    up, down, across, twin = at(z + 1, 0, c), at(z - 1, 0, c), at(z, 1, c), at(z, 0, 1 - c)
    waits, shared, crossing = [], [], {}

    def block(i, p):
        return g_ref.at[pl.ds(i * bands + p * w, w)]

    def send(dz, t, p, sends, recvs, to):
        i = at(z + dz, t, c)
        source = x_ref.at[pl.ds(p * w, w)] if dz == 0 and t == 0 else block(i, p)
        copy = remote(source, block(i, p), sends, recvs, lat=to)
        copy.start()
        waits.append(copy)

    def arrive(dz, t, cc, p, sends, recvs, peer):
        i = at(z + dz, t, cc)
        remote(block(i, p), block(i, p), sends, recvs, lat=peer).wait_recv()

    def limits(t, p):
        return (half, nz - 1 - half) if (t + p) % 2 == 0 else (nz - 1 - half, half)

    def hop(d, p, t, s):
        if s <= limits(t, p)[d]:
            if d == 0:
                send(1 - s, t, p, us.at[p, t, s - 1], ur.at[p, t, s - 1], up)
            else:
                send(s - 1, t, p, ds.at[p, t, s - 1], dr.at[p, t, s - 1], down)

    def landed(d, p, t, s):
        if d == 0:
            arrive(-s, t, c, p, us.at[p, t, s - 1], ur.at[p, t, s - 1], down)
        else:
            arrive(s, t, c, p, ds.at[p, t, s - 1], dr.at[p, t, s - 1], up)
        hop(d, p, t, s + 1)

    def share(dz, t, p):
        k = len(shared)
        shared.append((dz, t, p))
        send(dz, t, p, cs.at[k], cr.at[k], twin)

    def cross(dz, p):
        k = len(crossing)
        crossing[dz, p] = k
        send(dz, 0, p, ys.at[k], yr.at[k], across)

    def over(s):
        for p in range(n):
            for dz in (0,) if s == 0 else (-s, s):
                k = crossing[dz, p]
                arrive(dz, 1, c, p, ys.at[k], yr.at[k], across)
                if dz == -near:
                    hop(0, p, 1, near + 1)
                if dz == near:
                    hop(1, p, 1, near + 1)
                share(dz, 1, p)

    def own(s):
        for p in range(n):
            for d in range(2):
                if s <= limits(0, p)[d]:
                    dz = s if d else -s
                    landed(d, p, 0, s)
                    if s <= near:
                        cross(dz, p)
                    share(dz, 0, p)

    def far(s):
        for p in range(n):
            for d in range(2):
                if s <= limits(1, p)[d]:
                    landed(d, p, 1, s)
                    share(s if d else -s, 1, p)

    for p in range(n):
        cross(0, p)
        hop(0, p, 0, 1)
        hop(1, p, 0, 1)
    for p in range(n):
        share(0, 0, p)
    g_ref[pl.ds(lat * bands, bands)] = x_ref[...]
    between()
    for s in range(half):
        own(s + 1)
        if s <= near:
            over(s)
        else:
            far(s)
    far(half)
    for k, (dz, t, p) in enumerate(shared):
        arrive(dz, t, 1 - c, p, cs.at[k], cr.at[k], twin)
    return waits


def whole_kernel(
    nlat, nlon, block_keys, slot_ref, rows_ref, xt_ref, conv_in, wq_in, wk_in, wv_in, wo_in, area_in, out_ref,
    conv_ref, wq_ref, wk_ref, wv_ref, wo_ref, area_ref, load,
    g_ref, x_ref, ext, taps, pick, q_ref, kv_ref, e_ref, qa, stage, held,
    hsend, hrecv, ys, yr, us, ur, ds, dr, cs, cr, qsend, qrecv, osend, orecv,
):
    loads = [
        pltpu.make_async_copy(source, target, load.at[i])
        for i, (source, target) in enumerate((
            (conv_in, conv_ref), (area_in, area_ref), (wk_in, wk_ref),
            (wv_in, wv_ref), (wq_in, wq_ref), (wo_in, wo_ref),
        ))
    ]
    for copy in loads:
        copy.start()
    lat = lax.axis_index("lat")
    lon = lax.axis_index("lon")
    nz = nlat // 4
    high, cols, channels = xt_ref.shape
    bands, wide = x_ref.shape[0], x_ref.shape[1]
    z, yh, c = lat // 4, (lat // 2) % 2, lat % 2
    north, south = (lat + nlat - 1) % nlat, (lat + 1) % nlat
    west, east = (lon + nlon - 1) % nlon, (lon + 1) % nlon
    around = [(lon + k) % nlon for k in range(1, nlon)]
    column = z * 4 + yh * 2
    greet(
        [{"lat": p} for p in (
            ((z + 1) % nz) * 4 + yh * 2 + c,
            ((z + nz - 1) % nz) * 4 + yh * 2 + c,
            z * 4 + (1 - yh) * 2 + c,
            column + 1 - c,
            north, south,
        )]
        + [{"lon": p} for p in around]
        + [{"lat": a, "lon": b} for a in (north, south) for b in (west, east)]
    )
    strip = 16
    body, edge = pl.ds(0, cols), pl.ds(cols, strip)
    inner = pl.ds(cols - strip, strip)
    first, last = pl.ds(0, 2), pl.ds(high - 2, 2)
    below, above = pl.ds(0, 2), pl.ds(high + 2, 2)
    halo = [
        remote(xt_ref.at[last], ext.at[below, body], hsend.at[0], hrecv.at[0], lat=south),
        remote(xt_ref.at[first], ext.at[above, body], hsend.at[1], hrecv.at[1], lat=north),
        remote(xt_ref.at[:, inner], ext.at[pl.ds(2, high), edge], hsend.at[2], hrecv.at[2], lon=east),
        remote(xt_ref.at[last, inner], ext.at[below, edge], hsend.at[3], hrecv.at[3], lat=south, lon=east),
        remote(xt_ref.at[first, inner], ext.at[above, edge], hsend.at[4], hrecv.at[4], lat=north, lon=east),
    ]
    for copy in halo:
        copy.start()
    ext[2 : high + 2, 0:cols, :] = xt_ref[...]
    at_row = lax.broadcasted_iota(jnp.int32, (3 * wide, cols + strip), 0)
    at_col = lax.broadcasted_iota(jnp.int32, (3 * wide, cols + strip), 1)
    target = 2 * (at_row % wide) + at_row // wide - 1
    target = jnp.where(target < 0, cols + strip - 1, target)
    pickup = jnp.where(at_col == target, 1.0, 0.0).astype(jnp.bfloat16)
    for copy in halo:
        copy.wait_recv()
    keep_low = jnp.where(lat > 0, 1.0, 0.0)
    keep_high = jnp.where(lat < nlat - 1, 1.0, 0.0)
    for r in range(high + 4):
        tap = jnp.dot(pickup, ext[r], preferred_element_type=jnp.float32)
        if r < 2:
            tap = tap * keep_low
        if r >= high + 2:
            tap = tap * keep_high
        taps[r] = tap.astype(jnp.bfloat16)
    loads[0].wait()
    raw = jnp.zeros((bands * wide, D), jnp.float32)
    for k in range(rows_ref.shape[1]):
        found = [taps[2 * i + 2 + rows_ref[i, k]] for i in range(bands)]
        for t in range(3):
            part = jnp.concatenate([f[t * wide : (t + 1) * wide] for f in found], axis=0)
            raw = raw + jnp.dot(part, conv_ref[k, t], preferred_element_type=jnp.float32)
    factor = lax.rsqrt(jnp.mean(raw * raw, axis=-1, keepdims=True) + 1e-06)
    x_ref[...] = (raw * factor).astype(jnp.bfloat16).reshape(bands, wide, D)
    for copy in halo:
        copy.wait_send()

    def between():
        for copy in loads[1:]:
            copy.wait()
        e_ref[...] = jnp.broadcast_to(
            area_ref[...][:, None, :], (nlat * bands, wide, 128)
        ).reshape(e_ref.shape).astype(jnp.bfloat16)

    waits = ring(nz, NEAR, PIECES, x_ref, g_ref, (ys, yr, us, ur, ds, dr, cs, cr), between)
    chosen = g_ref[slot_ref[lat]]
    pick[...] = chosen
    q_ref[lon] = chosen
    for copy in waits:
        copy.wait_send()
    copies = []
    for k, peer in enumerate(around):
        copy = remote(pick, q_ref.at[lon], qsend.at[k], qrecv.at[k], lon=peer)
        copy.start()
        copies.append(copy)
    group = 8

    def project(i, carry):
        rows = g_ref[pl.ds(i * group, group)].reshape(group * wide, D)
        for j, w_ref in enumerate((wk_ref, wv_ref)):
            kv_ref[pl.ds(pl.multiple_of(i * group * wide, group * wide), group * wide), j * D : (j + 1) * D] = (
                jnp.dot(rows, w_ref[...], preferred_element_type=jnp.float32).astype(jnp.bfloat16)
            )
        return carry

    lax.fori_loop(0, g_ref.shape[0] // group, project, 0)

    outgoing = []
    for first_step in range(1, nlon + 1, 2):
        pair = (first_step, first_step + 1)
        for step in pair:
            if step < nlon:
                slot = (lon + step) % nlon
                k = nlon - step
                remote(pick, q_ref.at[slot], qsend.at[k - 1], qrecv.at[k - 1], lon=slot).wait_recv()
        mine = attend(
            jnp.concatenate([q_ref[(lon + step) % nlon] for step in pair], axis=0),
            wq_ref, kv_ref, e_ref, qa, block_keys,
        )
        for i, step in enumerate(pair):
            part = mine[i * wide : (i + 1) * wide]
            if step < nlon:
                stage[step - 1] = part
                peer = (lon + step) % nlon
                copy = remote(stage.at[step - 1], held.at[lon], osend.at[step - 1], orecv.at[step - 1], lon=peer)
                copy.start()
                outgoing.append(copy)
            else:
                held[lon] = part
    for k in range(1, nlon):
        slot = (lon + nlon - k) % nlon
        remote(stage.at[k - 1], held.at[slot], osend.at[k - 1], orecv.at[k - 1], lon=slot).wait_recv()
    out_ref[...] = merge(held, wo_ref, nlon)
    for copy in copies + outgoing:
        copy.wait_send()


def attend(features, wq_ref, kv_ref, e_ref, qa, block_keys):
    count = features.shape[0]
    rows = 2 * count
    q = jnp.dot(features, wq_ref[...], preferred_element_type=jnp.float32)
    q = q.astype(jnp.bfloat16).astype(jnp.float32) * (1.0 / math.sqrt(D // H))
    lane = lax.broadcasted_iota(jnp.int32, (count, 128), 1)
    marks = jnp.where(lax.broadcasted_iota(jnp.int32, (rows, 128), 1) < 3, 1.0, 0.0)
    tall = lax.broadcasted_iota(jnp.int32, (count, 128), 1)
    tail = jnp.zeros((count, 128), jnp.float32)
    for p in range(2):
        qp = q[:, p * 128 : (p + 1) * 128]
        qa[p, 0:count, 0:128] = jnp.where(lane < 64, qp, 0.0).astype(jnp.bfloat16)
        qa[p, count:rows, 0:128] = jnp.where(lane >= 64, qp, 0.0).astype(jnp.bfloat16)
        qa[p, :, 128:256] = marks.astype(jnp.bfloat16)
    top = [jnp.full((rows, 1), -1e30, jnp.float32)] * 2
    total = [jnp.zeros((rows, D), jnp.float32)] * 2
    for i in range(kv_ref.shape[0] // block_keys):
        keys = pl.ds(i * block_keys, block_keys)
        extra = e_ref[keys, :]
        for p in range(2):
            keyed = jnp.concatenate([kv_ref[keys, p * 128 : (p + 1) * 128], extra], axis=1)
            valued = jnp.concatenate([kv_ref[keys, D + p * 128 : D + (p + 1) * 128], extra], axis=1)
            s = lax.dot_general(
                qa[p], keyed, (((1,), (1,)), ((), ())), preferred_element_type=jnp.float32
            )
            best = jnp.maximum(top[p], jnp.max(s, axis=1, keepdims=True))
            w = jnp.exp(s - best).astype(jnp.bfloat16)
            update = jnp.dot(w, valued, preferred_element_type=jnp.float32)
            total[p] = update if i == 0 else total[p] * jnp.exp(top[p] - best) + update
            top[p] = best
    mixed = []
    for p in range(2):
        sums = total[p][:, 131:132]
        scaled = total[p][:, 0:128] / sums
        logs = top[p] + jnp.log(sums)
        mixed.append(jnp.where(lane < 64, scaled[0:count], scaled[count:rows]))
        for side in range(2):
            for t, piece in enumerate(split3(logs[side * count : (side + 1) * count])):
                tail = jnp.where(tall == 3 * (2 * p + side) + t, piece.astype(jnp.float32), tail)
    return jnp.concatenate(mixed + [tail], axis=1).astype(jnp.bfloat16)


def merge(held, w_ref, nlon):
    rows = held.shape[1]
    logs = []
    for i in range(nlon):
        tail = held[i, :, D : D + 128].astype(jnp.float32)
        logs.append([jnp.sum(tail[:, 3 * h : 3 * h + 3], axis=1, keepdims=True) for h in range(H)])
    head = lax.broadcasted_iota(jnp.int32, (rows, D), 1) // (D // H)
    top = [functools.reduce(jnp.maximum, [logs[i][h] for i in range(nlon)]) for h in range(H)]
    share = [[jnp.exp(logs[i][h] - top[h]) for h in range(H)] for i in range(nlon)]
    total = [1.0 / sum(share[i][h] for i in range(nlon)) for h in range(H)]
    mixed = jnp.zeros((rows, D), jnp.float32)
    for i in range(nlon):
        factor = jnp.zeros((rows, D), jnp.float32)
        for h in range(H):
            factor = jnp.where(head == h, share[i][h] * total[h], factor)
        mixed = mixed + factor * held[i, :, 0:D].astype(jnp.float32)
    return jnp.dot(
        mixed.astype(jnp.bfloat16), w_ref[...], preferred_element_type=jnp.float32
    ).astype(jnp.bfloat16)


def whole(window_bands, support_rows, state_field, conv_weight, w_query, w_key, w_value, w_out):
    nlat, nlon = lax.axis_size("lat"), lax.axis_size("lon")
    bands = support_rows.shape[0]
    channels, high, cols = state_field.shape
    wide = cols // 2
    v = pl.BlockSpec(memory_space=pltpu.VMEM)
    s = pl.BlockSpec(memory_space=pltpu.SMEM)
    far = pl.BlockSpec(memory_space=pl.ANY)
    dma = pltpu.SemaphoreType.DMA
    half = jnp.bfloat16
    n, nz, total = PIECES, nlat // 4, nlat * bands
    ring_sems = [dma(((2 * NEAR + 1) * n,))] * 2 + [dma((n, 2, nz // 2))] * 4 + [dma((2 * nz * n,))] * 2
    return pl.pallas_call(
        functools.partial(whole_kernel, nlat, nlon, BLOCK_KEYS),
        out_shape=jax.ShapeDtypeStruct((wide, D), half),
        in_specs=[s, s, v] + [far] * 6,
        out_specs=v,
        scratch_shapes=[
            pltpu.VMEM(conv_weight.shape, half),
            pltpu.VMEM((D, D), half), pltpu.VMEM((D, D), half),
            pltpu.VMEM((D, D), half), pltpu.VMEM((D, D), half),
            pltpu.VMEM((total, 128), jnp.float32),
            dma((6,)),
            pltpu.VMEM((total, wide, D), half),
            pltpu.VMEM((bands, wide, D), half),
            pltpu.VMEM((high + 4, cols + 16, channels), half),
            pltpu.VMEM((high + 4, 3 * wide, channels), half),
            pltpu.VMEM((wide, D), half),
            pltpu.VMEM((nlon, wide, D), half),
            pltpu.VMEM((total * wide, 2 * D), half),
            pltpu.VMEM((total * wide, 128), half),
            pltpu.VMEM((2, 4 * wide, D), half),
            pltpu.VMEM((nlon - 1, wide, D + 128), half),
            pltpu.VMEM((nlon, wide, D + 128), half),
            dma((5,)), dma((5,)),
        ] + ring_sems + [dma((nlon - 1,))] * 4,
        compiler_params=pltpu.CompilerParams(
            collective_id=0, has_side_effects=True, vmem_limit_bytes=60 * 1024 * 1024
        ),
        name="whole",
    )(
        window_bands, support_rows, jnp.transpose(state_field, (1, 2, 0)), conv_weight,
        w_query, w_key, w_value, w_out, jnp.asarray(area_table(total)),
    )


def split3(x):
    a = x.astype(jnp.bfloat16)
    r = x - a.astype(jnp.float32)
    b = r.astype(jnp.bfloat16)
    c = (r - b.astype(jnp.float32)).astype(jnp.bfloat16)
    return a, b, c

def area_table(nlat):
    c = (np.arange(nlat, dtype=np.float64) + 0.5) * (math.pi / nlat) - math.pi/2
    a = np.log(np.cos(c)).astype(np.float32)
    t = np.zeros((nlat, 128), np.float32)
    hi = a.astype(jnp.bfloat16).astype(np.float32)
    r = a - hi; mid = r.astype(jnp.bfloat16).astype(np.float32)
    lo = (r-mid).astype(jnp.bfloat16).astype(np.float32)
    t[:,0]=hi; t[:,1]=mid; t[:,2]=lo; t[:,3:6]=1.0
    return t

def per_device(
    state_field, support_rows, window_bands, conv_weight, w_query, w_key, w_value, w_out
):
    lon_tile = state_field.shape[2] // 2
    result = whole(
        window_bands, support_rows, state_field, conv_weight, w_query, w_key, w_value, w_out
    )
    return result.reshape(1, lon_tile, D)


def solution(mesh):
    return jax.shard_map(
        per_device,
        mesh=mesh,
        in_specs=(P(None, "lat", "lon"), P("lat", None), P(), P(), P(), P(), P(), P()),
        out_specs=P("lat", "lon", None),
        check_vma=False,
    )
```

```python
import functools
import math

import jax
import jax.numpy as jnp
import numpy as np
from jax import lax
from jax.experimental import pallas as pl
from jax.experimental.pallas import tpu as pltpu
from jax.sharding import PartitionSpec as P

D = 256
H = 4
NEAR = 1
PIECES = 2
BLOCK_KEYS = 2048


def remote(src, dst, send, recv, **where):
    return pltpu.make_async_remote_copy(
        src_ref=src, dst_ref=dst, send_sem=send, recv_sem=recv,
        device_id=where, device_id_type=pl.DeviceIdType.MESH)


def greet(peers):
    barrier = pltpu.get_barrier_semaphore()
    for peer in peers:
        pl.semaphore_signal(barrier, inc=1, device_id=peer, device_id_type=pl.DeviceIdType.MESH)
    pl.semaphore_wait(barrier, len(peers))


def ring(nz, near, n, x_ref, g_ref, sems, between):
    ys, yr, us, ur, ds, dr, cs, cr = sems
    bands = x_ref.shape[0]
    w = bands // n
    half = nz // 2
    lat = lax.axis_index("lat")
    z, yh, c = lat // 4, (lat // 2) % 2, lat % 2

    def at(zz, t, cc):
        return ((zz + nz) % nz) * 4 + (yh if t == 0 else 1 - yh) * 2 + cc

    up, down, across, twin = at(z + 1, 0, c), at(z - 1, 0, c), at(z, 1, c), at(z, 0, 1 - c)
    waits, shared, crossing = [], [], {}

    def block(i, p):
        return g_ref.at[pl.ds(i * bands + p * w, w)]

    def send(dz, t, p, sends, recvs, to):
        i = at(z + dz, t, c)
        source = x_ref.at[pl.ds(p * w, w)] if dz == 0 and t == 0 else block(i, p)
        copy = remote(source, block(i, p), sends, recvs, lat=to)
        copy.start()
        waits.append(copy)

    def arrive(dz, t, cc, p, sends, recvs, peer):
        i = at(z + dz, t, cc)
        remote(block(i, p), block(i, p), sends, recvs, lat=peer).wait_recv()

    def limits(t, p):
        return (half, nz - 1 - half) if (t + p) % 2 == 0 else (nz - 1 - half, half)

    def hop(d, p, t, s):
        if s <= limits(t, p)[d]:
            if d == 0:
                send(1 - s, t, p, us.at[p, t, s - 1], ur.at[p, t, s - 1], up)
            else:
                send(s - 1, t, p, ds.at[p, t, s - 1], dr.at[p, t, s - 1], down)

    def landed(d, p, t, s):
        if d == 0:
            arrive(-s, t, c, p, us.at[p, t, s - 1], ur.at[p, t, s - 1], down)
        else:
            arrive(s, t, c, p, ds.at[p, t, s - 1], dr.at[p, t, s - 1], up)
        hop(d, p, t, s + 1)

    def share(dz, t, p):
        k = len(shared)
        shared.append((dz, t, p))
        send(dz, t, p, cs.at[k], cr.at[k], twin)

    def cross(dz, p):
        k = len(crossing)
        crossing[dz, p] = k
        send(dz, 0, p, ys.at[k], yr.at[k], across)

    def over(s):
        for p in range(n):
            for dz in (0,) if s == 0 else (-s, s):
                k = crossing[dz, p]
                arrive(dz, 1, c, p, ys.at[k], yr.at[k], across)
                if dz == -near:
                    hop(0, p, 1, near + 1)
                if dz == near:
                    hop(1, p, 1, near + 1)
                share(dz, 1, p)

    def own(s):
        for p in range(n):
            for d in range(2):
                if s <= limits(0, p)[d]:
                    dz = s if d else -s
                    landed(d, p, 0, s)
                    if s <= near:
                        cross(dz, p)
                    share(dz, 0, p)

    def far(s):
        for p in range(n):
            for d in range(2):
                if s <= limits(1, p)[d]:
                    landed(d, p, 1, s)
                    share(s if d else -s, 1, p)

    for p in range(n):
        cross(0, p)
        hop(0, p, 0, 1)
        hop(1, p, 0, 1)
    for p in range(n):
        share(0, 0, p)
    g_ref[pl.ds(lat * bands, bands)] = x_ref[...]
    between()
    for s in range(half):
        own(s + 1)
        if s <= near:
            over(s)
        else:
            far(s)
    far(half)
    for k, (dz, t, p) in enumerate(shared):
        arrive(dz, t, 1 - c, p, cs.at[k], cr.at[k], twin)
    return waits


def whole_kernel(
    nlat, nlon, block_keys, slot_ref, rows_ref, xt_in, conv_in, wq_in, wk_in, wv_in, wo_in, area_in, out_ref,
    conv_ref, wq_ref, wk_ref, wv_ref, wo_ref, area_ref, load,
    g_ref, x_ref, ext, taps, pick, q_ref, kv_ref, e_ref, qa, stage, held,
    hsend, hrecv, ys, yr, us, ur, ds, dr, cs, cr, qsend, qrecv, osend, orecv,
):
    loads = [
        pltpu.make_async_copy(source, target, load.at[i])
        for i, (source, target) in enumerate((
            (conv_in, conv_ref), (area_in, area_ref), (wk_in, wk_ref),
            (wv_in, wv_ref), (wq_in, wq_ref), (wo_in, wo_ref),
        ))
    ]
    for copy in loads:
        copy.start()
    lat = lax.axis_index("lat")
    lon = lax.axis_index("lon")
    nz = nlat // 4
    high, cols, channels = xt_in.shape
    state = pltpu.make_async_copy(xt_in, ext.at[pl.ds(2, high), pl.ds(0, cols)], load.at[6])
    state.start()
    bands, wide = x_ref.shape[0], x_ref.shape[1]
    z, yh, c = lat // 4, (lat // 2) % 2, lat % 2
    north, south = (lat + nlat - 1) % nlat, (lat + 1) % nlat
    west, east = (lon + nlon - 1) % nlon, (lon + 1) % nlon
    around = [(lon + k) % nlon for k in range(1, nlon)]
    column = z * 4 + yh * 2
    greet(
        [{"lat": p} for p in (
            ((z + 1) % nz) * 4 + yh * 2 + c,
            ((z + nz - 1) % nz) * 4 + yh * 2 + c,
            z * 4 + (1 - yh) * 2 + c,
            column + 1 - c,
            north, south,
        )]
        + [{"lon": p} for p in around]
        + [{"lat": a, "lon": b} for a in (north, south) for b in (west, east)]
    )
    strip = 16
    body, edge = pl.ds(0, cols), pl.ds(cols, strip)
    inner = pl.ds(cols - strip, strip)
    first, last = pl.ds(0, 2), pl.ds(high - 2, 2)
    below, above = pl.ds(0, 2), pl.ds(high + 2, 2)
    halo = [
        remote(xt_in.at[last], ext.at[below, body], hsend.at[0], hrecv.at[0], lat=south),
        remote(xt_in.at[first], ext.at[above, body], hsend.at[1], hrecv.at[1], lat=north),
        remote(xt_in.at[:, inner], ext.at[pl.ds(2, high), edge], hsend.at[2], hrecv.at[2], lon=east),
        remote(xt_in.at[last, inner], ext.at[below, edge], hsend.at[3], hrecv.at[3], lat=south, lon=east),
        remote(xt_in.at[first, inner], ext.at[above, edge], hsend.at[4], hrecv.at[4], lat=north, lon=east),
    ]
    for copy in halo:
        copy.start()
    at_row = lax.broadcasted_iota(jnp.int32, (3 * wide, cols), 0)
    at_col = lax.broadcasted_iota(jnp.int32, (3 * wide, cols), 1)
    target = 2 * (at_row % wide) + at_row // wide - 1
    pickup = jnp.where(at_col == target, 1.0, 0.0).astype(jnp.bfloat16)
    state.wait()

    def tapped(r):
        return jnp.dot(pickup, ext[r, 0:cols, :], preferred_element_type=jnp.float32)

    for r in range(2, high + 2):
        taps[r] = tapped(r).astype(jnp.bfloat16)
    for copy in halo:
        copy.wait_recv()
    keep_low = jnp.where(lat > 0, 1.0, 0.0)
    keep_high = jnp.where(lat < nlat - 1, 1.0, 0.0)
    for r in range(high + 4):
        brink = ext[r, cols + strip - 1 : cols + strip, :].astype(jnp.float32)
        if r < 2 or r >= high + 2:
            keep = keep_low if r < 2 else keep_high
            taps[r] = (tapped(r) * keep).astype(jnp.bfloat16)
            brink = brink * keep
        taps[r, 0:1, :] = brink.astype(jnp.bfloat16)
    loads[0].wait()
    raw = jnp.zeros((bands * wide, D), jnp.float32)
    for k in range(rows_ref.shape[1]):
        found = [taps[2 * i + 2 + rows_ref[i, k]] for i in range(bands)]
        for t in range(3):
            part = jnp.concatenate([f[t * wide : (t + 1) * wide] for f in found], axis=0)
            raw = raw + jnp.dot(part, conv_ref[k, t], preferred_element_type=jnp.float32)
    factor = lax.rsqrt(jnp.mean(raw * raw, axis=-1, keepdims=True) + 1e-06)
    x_ref[...] = (raw * factor).astype(jnp.bfloat16).reshape(bands, wide, D)
    for copy in halo:
        copy.wait_send()

    def between():
        for copy in loads[1:]:
            copy.wait()
        e_ref[...] = jnp.broadcast_to(
            area_ref[...][:, None, :], (nlat * bands, wide, 128)
        ).reshape(e_ref.shape).astype(jnp.bfloat16)

    waits = ring(nz, NEAR, PIECES, x_ref, g_ref, (ys, yr, us, ur, ds, dr, cs, cr), between)
    chosen = g_ref[slot_ref[lat]]
    pick[...] = chosen
    q_ref[lon] = chosen
    copies = list(waits)
    for k, peer in enumerate(around):
        copy = remote(pick, q_ref.at[lon], qsend.at[k], qrecv.at[k], lon=peer)
        copy.start()
        copies.append(copy)
    group = 8

    def project(i, carry):
        rows = g_ref[pl.ds(i * group, group)].reshape(group * wide, D)
        for j, w_ref in enumerate((wk_ref, wv_ref)):
            kv_ref[pl.ds(pl.multiple_of(i * group * wide, group * wide), group * wide), j * D : (j + 1) * D] = (
                jnp.dot(rows, w_ref[...], preferred_element_type=jnp.float32).astype(jnp.bfloat16)
            )
        return carry

    lax.fori_loop(0, g_ref.shape[0] // group, project, 0)

    outgoing = []
    for first_step in range(0, nlon, 2):
        pair = (first_step, first_step + 1)
        for step in pair:
            if step > 0:
                slot = (lon + step) % nlon
                k = nlon - step
                remote(pick, q_ref.at[slot], qsend.at[k - 1], qrecv.at[k - 1], lon=slot).wait_recv()
        mine = attend(
            jnp.concatenate([q_ref[(lon + step) % nlon] for step in pair], axis=0),
            wq_ref, kv_ref, e_ref, qa, block_keys,
        )
        for i, step in enumerate(pair):
            part = mine[i * wide : (i + 1) * wide]
            if step > 0:
                stage[step - 1] = part
                peer = (lon + step) % nlon
                copy = remote(stage.at[step - 1], held.at[lon], osend.at[step - 1], orecv.at[step - 1], lon=peer)
                copy.start()
                outgoing.append(copy)
            else:
                held[lon] = part
    for k in range(1, nlon):
        slot = (lon + nlon - k) % nlon
        remote(stage.at[k - 1], held.at[slot], osend.at[k - 1], orecv.at[k - 1], lon=slot).wait_recv()
    out_ref[...] = merge(held, wo_ref, nlon)
    for copy in copies + outgoing:
        copy.wait_send()


def attend(features, wq_ref, kv_ref, e_ref, qa, block_keys):
    count = features.shape[0]
    rows = 2 * count
    q = jnp.dot(features, wq_ref[...], preferred_element_type=jnp.float32)
    q = q.astype(jnp.bfloat16).astype(jnp.float32) * (1.0 / math.sqrt(D // H))
    lane = lax.broadcasted_iota(jnp.int32, (count, 128), 1)
    marks = jnp.where(lax.broadcasted_iota(jnp.int32, (rows, 128), 1) < 3, 1.0, 0.0)
    tall = lax.broadcasted_iota(jnp.int32, (count, 128), 1)
    tail = jnp.zeros((count, 128), jnp.float32)
    for p in range(2):
        qp = q[:, p * 128 : (p + 1) * 128]
        qa[p, 0:count, 0:128] = jnp.where(lane < 64, qp, 0.0).astype(jnp.bfloat16)
        qa[p, count:rows, 0:128] = jnp.where(lane >= 64, qp, 0.0).astype(jnp.bfloat16)
        qa[p, :, 128:256] = marks.astype(jnp.bfloat16)
    top = [jnp.full((rows, 1), -1e30, jnp.float32)] * 2
    total = [jnp.zeros((rows, D), jnp.float32)] * 2
    for i in range(kv_ref.shape[0] // block_keys):
        keys = pl.ds(i * block_keys, block_keys)
        extra = e_ref[keys, :]
        for p in range(2):
            keyed = jnp.concatenate([kv_ref[keys, p * 128 : (p + 1) * 128], extra], axis=1)
            valued = jnp.concatenate([kv_ref[keys, D + p * 128 : D + (p + 1) * 128], extra], axis=1)
            s = lax.dot_general(
                qa[p], keyed, (((1,), (1,)), ((), ())), preferred_element_type=jnp.float32
            )
            best = jnp.maximum(top[p], jnp.max(s, axis=1, keepdims=True))
            w = jnp.exp(s - best).astype(jnp.bfloat16)
            update = jnp.dot(w, valued, preferred_element_type=jnp.float32)
            total[p] = update if i == 0 else total[p] * jnp.exp(top[p] - best) + update
            top[p] = best
    mixed = []
    for p in range(2):
        sums = total[p][:, 131:132]
        scaled = total[p][:, 0:128] / sums
        logs = top[p] + jnp.log(sums)
        mixed.append(jnp.where(lane < 64, scaled[0:count], scaled[count:rows]))
        for side in range(2):
            for t, piece in enumerate(split3(logs[side * count : (side + 1) * count])):
                tail = jnp.where(tall == 3 * (2 * p + side) + t, piece.astype(jnp.float32), tail)
    return jnp.concatenate(mixed + [tail], axis=1).astype(jnp.bfloat16)


def merge(held, w_ref, nlon):
    rows = held.shape[1]
    logs = []
    for i in range(nlon):
        tail = held[i, :, D : D + 128].astype(jnp.float32)
        logs.append([jnp.sum(tail[:, 3 * h : 3 * h + 3], axis=1, keepdims=True) for h in range(H)])
    head = lax.broadcasted_iota(jnp.int32, (rows, D), 1) // (D // H)
    top = [functools.reduce(jnp.maximum, [logs[i][h] for i in range(nlon)]) for h in range(H)]
    share = [[jnp.exp(logs[i][h] - top[h]) for h in range(H)] for i in range(nlon)]
    total = [1.0 / sum(share[i][h] for i in range(nlon)) for h in range(H)]
    mixed = jnp.zeros((rows, D), jnp.float32)
    for i in range(nlon):
        factor = jnp.zeros((rows, D), jnp.float32)
        for h in range(H):
            factor = jnp.where(head == h, share[i][h] * total[h], factor)
        mixed = mixed + factor * held[i, :, 0:D].astype(jnp.float32)
    return jnp.dot(
        mixed.astype(jnp.bfloat16), w_ref[...], preferred_element_type=jnp.float32
    ).astype(jnp.bfloat16)


def whole(window_bands, support_rows, state_field, conv_weight, w_query, w_key, w_value, w_out):
    nlat, nlon = lax.axis_size("lat"), lax.axis_size("lon")
    bands = support_rows.shape[0]
    channels, high, cols = state_field.shape
    wide = cols // 2
    v = pl.BlockSpec(memory_space=pltpu.VMEM)
    s = pl.BlockSpec(memory_space=pltpu.SMEM)
    far = pl.BlockSpec(memory_space=pl.ANY)
    dma = pltpu.SemaphoreType.DMA
    half = jnp.bfloat16
    n, nz, total = PIECES, nlat // 4, nlat * bands
    ring_sems = [dma(((2 * NEAR + 1) * n,))] * 2 + [dma((n, 2, nz // 2))] * 4 + [dma((2 * nz * n,))] * 2
    return pl.pallas_call(
        functools.partial(whole_kernel, nlat, nlon, BLOCK_KEYS),
        out_shape=jax.ShapeDtypeStruct((wide, D), half),
        in_specs=[s, s] + [far] * 7,
        out_specs=v,
        scratch_shapes=[
            pltpu.VMEM(conv_weight.shape, half),
            pltpu.VMEM((D, D), half), pltpu.VMEM((D, D), half),
            pltpu.VMEM((D, D), half), pltpu.VMEM((D, D), half),
            pltpu.VMEM((total, 128), jnp.float32),
            dma((7,)),
            pltpu.VMEM((total, wide, D), half),
            pltpu.VMEM((bands, wide, D), half),
            pltpu.VMEM((high + 4, cols + 16, channels), half),
            pltpu.VMEM((high + 4, 3 * wide, channels), half),
            pltpu.VMEM((wide, D), half),
            pltpu.VMEM((nlon, wide, D), half),
            pltpu.VMEM((total * wide, 2 * D), half),
            pltpu.VMEM((total * wide, 128), half),
            pltpu.VMEM((2, 4 * wide, D), half),
            pltpu.VMEM((nlon - 1, wide, D + 128), half),
            pltpu.VMEM((nlon, wide, D + 128), half),
            dma((5,)), dma((5,)),
        ] + ring_sems + [dma((nlon - 1,))] * 4,
        compiler_params=pltpu.CompilerParams(
            collective_id=0, has_side_effects=True, vmem_limit_bytes=60 * 1024 * 1024
        ),
        name="whole",
    )(
        window_bands, support_rows, jnp.transpose(state_field, (1, 2, 0)), conv_weight,
        w_query, w_key, w_value, w_out, jnp.asarray(area_table(total)),
    )


def split3(x):
    a = x.astype(jnp.bfloat16)
    r = x - a.astype(jnp.float32)
    b = r.astype(jnp.bfloat16)
    c = (r - b.astype(jnp.float32)).astype(jnp.bfloat16)
    return a, b, c

def area_table(nlat):
    c = (np.arange(nlat, dtype=np.float64) + 0.5) * (math.pi / nlat) - math.pi/2
    a = np.log(np.cos(c)).astype(np.float32)
    t = np.zeros((nlat, 128), np.float32)
    hi = a.astype(jnp.bfloat16).astype(np.float32)
    r = a - hi; mid = r.astype(jnp.bfloat16).astype(np.float32)
    lo = (r-mid).astype(jnp.bfloat16).astype(np.float32)
    t[:,0]=hi; t[:,1]=mid; t[:,2]=lo; t[:,3:6]=1.0
    return t

def per_device(
    state_field, support_rows, window_bands, conv_weight, w_query, w_key, w_value, w_out
):
    lon_tile = state_field.shape[2] // 2
    result = whole(
        window_bands, support_rows, state_field, conv_weight, w_query, w_key, w_value, w_out
    )
    return result.reshape(1, lon_tile, D)


def solution(mesh):
    return jax.shard_map(
        per_device,
        mesh=mesh,
        in_specs=(P(None, "lat", "lon"), P("lat", None), P(), P(), P(), P(), P(), P()),
        out_specs=P("lat", "lon", None),
        check_vma=False,
    )
```

```python
import functools
import math

import jax
import jax.numpy as jnp
import numpy as np
from jax import lax
from jax.experimental import pallas as pl
from jax.experimental.pallas import tpu as pltpu
from jax.sharding import PartitionSpec as P

D = 256
H = 4
NEAR = 1
PIECES = 2
BLOCK_KEYS = 2048


def remote(src, dst, send, recv, **where):
    return pltpu.make_async_remote_copy(
        src_ref=src, dst_ref=dst, send_sem=send, recv_sem=recv,
        device_id=where, device_id_type=pl.DeviceIdType.MESH)


def greet(peers):
    barrier = pltpu.get_barrier_semaphore()
    for peer in peers:
        pl.semaphore_signal(barrier, inc=1, device_id=peer, device_id_type=pl.DeviceIdType.MESH)
    pl.semaphore_wait(barrier, len(peers))


def ring(nz, near, n, x_ref, g_ref, sems, between):
    ys, yr, us, ur, ds, dr, cs, cr = sems
    bands = x_ref.shape[0]
    w = bands // n
    half = nz // 2
    lat = lax.axis_index("lat")
    z, yh, c = lat // 4, (lat // 2) % 2, lat % 2

    def at(zz, t, cc):
        return ((zz + nz) % nz) * 4 + (yh if t == 0 else 1 - yh) * 2 + cc

    up, down, across, twin = at(z + 1, 0, c), at(z - 1, 0, c), at(z, 1, c), at(z, 0, 1 - c)
    waits, shared, crossing = [], [], {}

    def block(i, p):
        return g_ref.at[pl.ds(i * bands + p * w, w)]

    def send(dz, t, p, sends, recvs, to):
        i = at(z + dz, t, c)
        source = x_ref.at[pl.ds(p * w, w)] if dz == 0 and t == 0 else block(i, p)
        copy = remote(source, block(i, p), sends, recvs, lat=to)
        copy.start()
        waits.append(copy)

    def arrive(dz, t, cc, p, sends, recvs, peer):
        i = at(z + dz, t, cc)
        remote(block(i, p), block(i, p), sends, recvs, lat=peer).wait_recv()

    def limits(t, p):
        return (half, nz - 1 - half) if (t + p) % 2 == 0 else (nz - 1 - half, half)

    def hop(d, p, t, s):
        if s <= limits(t, p)[d]:
            if d == 0:
                send(1 - s, t, p, us.at[p, t, s - 1], ur.at[p, t, s - 1], up)
            else:
                send(s - 1, t, p, ds.at[p, t, s - 1], dr.at[p, t, s - 1], down)

    def landed(d, p, t, s):
        if d == 0:
            arrive(-s, t, c, p, us.at[p, t, s - 1], ur.at[p, t, s - 1], down)
        else:
            arrive(s, t, c, p, ds.at[p, t, s - 1], dr.at[p, t, s - 1], up)
        hop(d, p, t, s + 1)

    def share(dz, t, p):
        k = len(shared)
        shared.append((dz, t, p))
        send(dz, t, p, cs.at[k], cr.at[k], twin)

    def cross(dz, p):
        k = len(crossing)
        crossing[dz, p] = k
        send(dz, 0, p, ys.at[k], yr.at[k], across)

    def over(s):
        for p in range(n):
            for dz in (0,) if s == 0 else (-s, s):
                k = crossing[dz, p]
                arrive(dz, 1, c, p, ys.at[k], yr.at[k], across)
                if dz == -near:
                    hop(0, p, 1, near + 1)
                if dz == near:
                    hop(1, p, 1, near + 1)
                share(dz, 1, p)

    def own(s):
        for p in range(n):
            for d in range(2):
                if s <= limits(0, p)[d]:
                    dz = s if d else -s
                    landed(d, p, 0, s)
                    if s <= near:
                        cross(dz, p)
                    share(dz, 0, p)

    def far(s):
        for p in range(n):
            for d in range(2):
                if s <= limits(1, p)[d]:
                    landed(d, p, 1, s)
                    share(s if d else -s, 1, p)

    for p in range(n):
        cross(0, p)
        hop(0, p, 0, 1)
        hop(1, p, 0, 1)
    for p in range(n):
        share(0, 0, p)
    g_ref[pl.ds(lat * bands, bands)] = x_ref[...]
    between()
    for s in range(half):
        own(s + 1)
        if s <= near:
            over(s)
        else:
            far(s)
    far(half)
    for k, (dz, t, p) in enumerate(shared):
        arrive(dz, t, 1 - c, p, cs.at[k], cr.at[k], twin)
    return waits


def whole_kernel(
    nlat, nlon, block_keys, slot_ref, rows_ref, xt_in, conv_in, wq_in, wk_in, wv_in, area_in, out_ref,
    conv_ref, wq_ref, wk_ref, wv_ref, area_ref, load,
    g_ref, x_ref, ext, taps, pick, q_ref, kv_ref, e_ref, qa, stage, held,
    hsend, hrecv, ys, yr, us, ur, ds, dr, cs, cr, qsend, qrecv, osend, orecv,
):
    loads = [
        pltpu.make_async_copy(source, target, load.at[i])
        for i, (source, target) in enumerate((
            (conv_in, conv_ref), (area_in, area_ref), (wk_in, wk_ref),
            (wv_in, wv_ref), (wq_in, wq_ref),
        ))
    ]
    for copy in loads:
        copy.start()
    lat = lax.axis_index("lat")
    lon = lax.axis_index("lon")
    nz = nlat // 4
    high, cols, channels = xt_in.shape
    state = pltpu.make_async_copy(xt_in, ext.at[pl.ds(2, high), pl.ds(0, cols)], load.at[5])
    state.start()
    bands, wide = x_ref.shape[0], x_ref.shape[1]
    z, yh, c = lat // 4, (lat // 2) % 2, lat % 2
    north, south = (lat + nlat - 1) % nlat, (lat + 1) % nlat
    west, east = (lon + nlon - 1) % nlon, (lon + 1) % nlon
    around = [(lon + k) % nlon for k in range(1, nlon)]
    column = z * 4 + yh * 2
    greet(
        [{"lat": p} for p in (
            ((z + 1) % nz) * 4 + yh * 2 + c,
            ((z + nz - 1) % nz) * 4 + yh * 2 + c,
            z * 4 + (1 - yh) * 2 + c,
            column + 1 - c,
            north, south,
        )]
        + [{"lon": p} for p in around]
        + [{"lat": a, "lon": b} for a in (north, south) for b in (west, east)]
    )
    strip = 16
    body, edge = pl.ds(0, cols), pl.ds(cols, strip)
    inner = pl.ds(cols - strip, strip)
    first, last = pl.ds(0, 2), pl.ds(high - 2, 2)
    below, above = pl.ds(0, 2), pl.ds(high + 2, 2)
    halo = [
        remote(xt_in.at[last], ext.at[below, body], hsend.at[0], hrecv.at[0], lat=south),
        remote(xt_in.at[first], ext.at[above, body], hsend.at[1], hrecv.at[1], lat=north),
        remote(xt_in.at[:, inner], ext.at[pl.ds(2, high), edge], hsend.at[2], hrecv.at[2], lon=east),
        remote(xt_in.at[last, inner], ext.at[below, edge], hsend.at[3], hrecv.at[3], lat=south, lon=east),
        remote(xt_in.at[first, inner], ext.at[above, edge], hsend.at[4], hrecv.at[4], lat=north, lon=east),
    ]
    for copy in halo:
        copy.start()
    at_row = lax.broadcasted_iota(jnp.int32, (3 * wide, cols), 0)
    at_col = lax.broadcasted_iota(jnp.int32, (3 * wide, cols), 1)
    target = 2 * (at_row % wide) + at_row // wide - 1
    pickup = jnp.where(at_col == target, 1.0, 0.0).astype(jnp.bfloat16)
    state.wait()

    def tapped(r):
        return jnp.dot(pickup, ext[r, 0:cols, :], preferred_element_type=jnp.float32)

    for r in range(2, high + 2):
        taps[r] = tapped(r).astype(jnp.bfloat16)
    for copy in halo:
        copy.wait_recv()
    keep_low = jnp.where(lat > 0, 1.0, 0.0)
    keep_high = jnp.where(lat < nlat - 1, 1.0, 0.0)
    for r in range(high + 4):
        brink = ext[r, cols + strip - 1 : cols + strip, :].astype(jnp.float32)
        if r < 2 or r >= high + 2:
            keep = keep_low if r < 2 else keep_high
            taps[r] = (tapped(r) * keep).astype(jnp.bfloat16)
            brink = brink * keep
        taps[r, 0:1, :] = brink.astype(jnp.bfloat16)
    loads[0].wait()
    raw = jnp.zeros((bands * wide, D), jnp.float32)
    for k in range(rows_ref.shape[1]):
        found = [taps[2 * i + 2 + rows_ref[i, k]] for i in range(bands)]
        for t in range(3):
            part = jnp.concatenate([f[t * wide : (t + 1) * wide] for f in found], axis=0)
            raw = raw + jnp.dot(part, conv_ref[k, t], preferred_element_type=jnp.float32)
    factor = lax.rsqrt(jnp.mean(raw * raw, axis=-1, keepdims=True) + 1e-06)
    x_ref[...] = (raw * factor).astype(jnp.bfloat16).reshape(bands, wide, D)
    for copy in halo:
        copy.wait_send()

    def between():
        for copy in loads[1:]:
            copy.wait()
        e_ref[...] = jnp.broadcast_to(
            area_ref[...][:, None, :], (nlat * bands, wide, 128)
        ).reshape(e_ref.shape).astype(jnp.bfloat16)

    waits = ring(nz, NEAR, PIECES, x_ref, g_ref, (ys, yr, us, ur, ds, dr, cs, cr), between)
    chosen = g_ref[slot_ref[lat]]
    pick[...] = chosen
    q_ref[lon] = chosen
    copies = list(waits)
    for k, peer in enumerate(around):
        copy = remote(pick, q_ref.at[lon], qsend.at[k], qrecv.at[k], lon=peer)
        copy.start()
        copies.append(copy)
    group = 8

    def project(i, carry):
        rows = g_ref[pl.ds(i * group, group)].reshape(group * wide, D)
        for j, w_ref in enumerate((wk_ref, wv_ref)):
            kv_ref[pl.ds(pl.multiple_of(i * group * wide, group * wide), group * wide), j * D : (j + 1) * D] = (
                jnp.dot(rows, w_ref[...], preferred_element_type=jnp.float32).astype(jnp.bfloat16)
            )
        return carry

    lax.fori_loop(0, g_ref.shape[0] // group, project, 0)

    outgoing = []
    for first_step in range(1, nlon, 2):
        pair = (first_step, (first_step + 1) % nlon)
        for step in pair:
            if step > 0:
                slot = (lon + step) % nlon
                k = nlon - step
                remote(pick, q_ref.at[slot], qsend.at[k - 1], qrecv.at[k - 1], lon=slot).wait_recv()
        mine = attend(
            jnp.concatenate([q_ref[(lon + step) % nlon] for step in pair], axis=0),
            wq_ref, kv_ref, e_ref, qa, block_keys,
        )
        for i, step in enumerate(pair):
            part = mine[i * wide : (i + 1) * wide]
            if step > 0:
                stage[step - 1] = part
                peer = (lon + step) % nlon
                copy = remote(stage.at[step - 1], held.at[lon], osend.at[step - 1], orecv.at[step - 1], lon=peer)
                copy.start()
                outgoing.append(copy)
            else:
                held[lon] = part
    def ready(k):
        slot = (lon + nlon - k) % nlon
        if k > 0:
            remote(stage.at[k - 1], held.at[slot], osend.at[k - 1], orecv.at[k - 1], lon=slot).wait_recv()
        return slot

    out_ref[...] = merge(held, ready, nlon)
    for copy in copies + outgoing:
        copy.wait_send()


def attend(features, wq_ref, kv_ref, e_ref, qa, block_keys):
    count = features.shape[0]
    rows = 2 * count
    q = jnp.dot(features, wq_ref[...], preferred_element_type=jnp.float32)
    q = q.astype(jnp.bfloat16).astype(jnp.float32) * (1.0 / math.sqrt(D // H))
    lane = lax.broadcasted_iota(jnp.int32, (count, 128), 1)
    marks = jnp.where(lax.broadcasted_iota(jnp.int32, (rows, 128), 1) < 3, 1.0, 0.0)
    tall = lax.broadcasted_iota(jnp.int32, (count, 128), 1)
    tail = jnp.zeros((count, 128), jnp.float32)
    for p in range(2):
        qp = q[:, p * 128 : (p + 1) * 128]
        qa[p, 0:count, 0:128] = jnp.where(lane < 64, qp, 0.0).astype(jnp.bfloat16)
        qa[p, count:rows, 0:128] = jnp.where(lane >= 64, qp, 0.0).astype(jnp.bfloat16)
        qa[p, :, 128:256] = marks.astype(jnp.bfloat16)
    top = [jnp.full((rows, 1), -1e30, jnp.float32)] * 2
    total = [jnp.zeros((rows, D), jnp.float32)] * 2
    for i in range(kv_ref.shape[0] // block_keys):
        keys = pl.ds(i * block_keys, block_keys)
        extra = e_ref[keys, :]
        for p in range(2):
            keyed = jnp.concatenate([kv_ref[keys, p * 128 : (p + 1) * 128], extra], axis=1)
            valued = jnp.concatenate([kv_ref[keys, D + p * 128 : D + (p + 1) * 128], extra], axis=1)
            s = lax.dot_general(
                qa[p], keyed, (((1,), (1,)), ((), ())), preferred_element_type=jnp.float32
            )
            best = jnp.maximum(top[p], jnp.max(s, axis=1, keepdims=True))
            w = jnp.exp(s - best).astype(jnp.bfloat16)
            update = jnp.dot(w, valued, preferred_element_type=jnp.float32)
            total[p] = update if i == 0 else total[p] * jnp.exp(top[p] - best) + update
            top[p] = best
    mixed = []
    for p in range(2):
        sums = total[p][:, 131:132]
        scaled = total[p][:, 0:128] / sums
        logs = top[p] + jnp.log(sums)
        mixed.append(jnp.where(lane < 64, scaled[0:count], scaled[count:rows]))
        for side in range(2):
            for t, piece in enumerate(split3(logs[side * count : (side + 1) * count])):
                tail = jnp.where(tall == 3 * (2 * p + side) + t, piece.astype(jnp.float32), tail)
    return jnp.concatenate(mixed + [tail], axis=1).astype(jnp.bfloat16)


def merge(held, ready, nlon):
    rows = held.shape[1]
    logs, parts = [], []
    for i in range(nlon):
        slot = ready(i)
        tail = held[slot, :, D : D + 128].astype(jnp.float32)
        logs.append([jnp.sum(tail[:, 3 * h : 3 * h + 3], axis=1, keepdims=True) for h in range(H)])
        parts.append(slot)
    head = lax.broadcasted_iota(jnp.int32, (rows, D), 1) // (D // H)
    top = [functools.reduce(jnp.maximum, [logs[i][h] for i in range(nlon)]) for h in range(H)]
    share = [[jnp.exp(logs[i][h] - top[h]) for h in range(H)] for i in range(nlon)]
    total = [1.0 / sum(share[i][h] for i in range(nlon)) for h in range(H)]
    mixed = jnp.zeros((rows, D), jnp.float32)
    for i in range(nlon):
        factor = jnp.zeros((rows, D), jnp.float32)
        for h in range(H):
            factor = jnp.where(head == h, share[i][h] * total[h], factor)
        mixed = mixed + factor * held[parts[i], :, 0:D].astype(jnp.float32)
    return mixed.astype(jnp.bfloat16)


def whole(window_bands, support_rows, state_field, conv_weight, w_query, w_key, w_value):
    nlat, nlon = lax.axis_size("lat"), lax.axis_size("lon")
    bands = support_rows.shape[0]
    channels, high, cols = state_field.shape
    wide = cols // 2
    v = pl.BlockSpec(memory_space=pltpu.VMEM)
    s = pl.BlockSpec(memory_space=pltpu.SMEM)
    far = pl.BlockSpec(memory_space=pl.ANY)
    dma = pltpu.SemaphoreType.DMA
    half = jnp.bfloat16
    n, nz, total = PIECES, nlat // 4, nlat * bands
    ring_sems = [dma(((2 * NEAR + 1) * n,))] * 2 + [dma((n, 2, nz // 2))] * 4 + [dma((2 * nz * n,))] * 2
    return pl.pallas_call(
        functools.partial(whole_kernel, nlat, nlon, BLOCK_KEYS),
        out_shape=jax.ShapeDtypeStruct((wide, D), half),
        in_specs=[s, s] + [far] * 6,
        out_specs=v,
        scratch_shapes=[
            pltpu.VMEM(conv_weight.shape, half),
            pltpu.VMEM((D, D), half), pltpu.VMEM((D, D), half), pltpu.VMEM((D, D), half),
            pltpu.VMEM((total, 128), jnp.float32),
            dma((6,)),
            pltpu.VMEM((total, wide, D), half),
            pltpu.VMEM((bands, wide, D), half),
            pltpu.VMEM((high + 4, cols + 16, channels), half),
            pltpu.VMEM((high + 4, 3 * wide, channels), half),
            pltpu.VMEM((wide, D), half),
            pltpu.VMEM((nlon, wide, D), half),
            pltpu.VMEM((total * wide, 2 * D), half),
            pltpu.VMEM((total * wide, 128), half),
            pltpu.VMEM((2, 4 * wide, D), half),
            pltpu.VMEM((nlon - 1, wide, D + 128), half),
            pltpu.VMEM((nlon, wide, D + 128), half),
            dma((5,)), dma((5,)),
        ] + ring_sems + [dma((nlon - 1,))] * 4,
        compiler_params=pltpu.CompilerParams(
            collective_id=0, has_side_effects=True, vmem_limit_bytes=60 * 1024 * 1024
        ),
        name="whole",
    )(
        window_bands, support_rows, jnp.transpose(state_field, (1, 2, 0)), conv_weight,
        w_query, w_key, w_value, jnp.asarray(area_table(total)),
    )


def split3(x):
    a = x.astype(jnp.bfloat16)
    r = x - a.astype(jnp.float32)
    b = r.astype(jnp.bfloat16)
    c = (r - b.astype(jnp.float32)).astype(jnp.bfloat16)
    return a, b, c

def area_table(nlat):
    c = (np.arange(nlat, dtype=np.float64) + 0.5) * (math.pi / nlat) - math.pi/2
    a = np.log(np.cos(c)).astype(np.float32)
    t = np.zeros((nlat, 128), np.float32)
    hi = a.astype(jnp.bfloat16).astype(np.float32)
    r = a - hi; mid = r.astype(jnp.bfloat16).astype(np.float32)
    lo = (r-mid).astype(jnp.bfloat16).astype(np.float32)
    t[:,0]=hi; t[:,1]=mid; t[:,2]=lo; t[:,3:6]=1.0
    return t

def per_device(
    state_field, support_rows, window_bands, conv_weight, w_query, w_key, w_value, w_out
):
    lon_tile = state_field.shape[2] // 2
    attended = whole(
        window_bands, support_rows, state_field, conv_weight, w_query, w_key, w_value
    )
    result = jnp.dot(attended, w_out, preferred_element_type=jnp.float32).astype(jnp.bfloat16)
    return result.reshape(1, lon_tile, D)


def solution(mesh):
    return jax.shard_map(
        per_device,
        mesh=mesh,
        in_specs=(P(None, "lat", "lon"), P("lat", None), P(), P(), P(), P(), P(), P()),
        out_specs=P("lat", "lon", None),
        check_vma=False,
    )
```
